256 devices in a mesh: context: 32 (over y, z), head: 2 (over core), dp: 4 (over x).
Axes of the slice: x: 4, y: 4, z: 8, core: 2. Of those that a mesh axis runs over, the one named last changes fastest.
Arguments:
- lin_query: float32 [16384, 4096], P(('dp', 'context'), 'head'), parts along dimension 0, may hold values from -6 to 6
- lin_key: float32 [16384, 4096], P(('dp', 'context'), 'head'), parts along dimension 0, may hold values from -6 to 6
- lin_value: float32 [16384, 4096], P(('dp', 'context'), 'head'), parts along dimension 0, may hold values from -6 to 6
- lin_gate: float32 [16384, 4096], P(('dp', 'context'), 'head'), parts along dimension 0, may hold values from -8 to 8
- decay_rate: float32 [32, 16384], P('head', ('dp', 'context')), parts along dimension 1, may hold values from 0 to 1.5, as said below
- norm_gain: float32 [4096], P('head'), may hold values from 0.5 to 1.5
- sm_query: float32 [16384, 4096], P(('dp', 'context'), 'head'), parts along dimension 0, may hold values from -24 to 24
- sm_key: float32 [16384, 512], P(('dp', 'context'), 'head'), parts along dimension 0, may hold values from -24 to 24
- sm_value: float32 [16384, 512], P(('dp', 'context'), 'head'), parts along dimension 0, may hold values from -6 to 6
- doc_lengths: int32 [64], P('dp'), parts along dimension 0, may hold values from 1 to 3072, 4096 in all
Outputs:
- lin_out: float32 [16384, 4096], P(('dp', 'context'), 'head'), parts along dimension 0
- sm_out: float32 [16384, 4096], P(('dp', 'context'), 'head'), parts along dimension 0
The draws below stay inside these ranges and needn't reach their ends.
There are 4 independent parts, one for each index of `dp`. The reference program is written for one: setup_inputs(seed, part) draws one part's arguments, and reference() takes and returns one part's arrays. A program takes and returns all parts, laid end to end along the dimension named above; an argument that names none is the same for every part. Nothing has to cross between parts.
Inputs may be any that keep to these rules, and one draw needn't show every extreme that they name: `doc_lengths`: the 16 lengths sum to 4096 and the longest is exactly 3072. `decay_rate`: positive rates.
All inputs are finite; a program needn't handle non-finite values.
Results may differ from the reference program's by a relative error of at most 0.0003.
Values sent between devices are 32-bit elements; how exact they have to be, the bound alone decides.
No kernel may reach another device: no remote copies, remote signals or barrier semaphores. Data moves between devices by JAX's collectives and lax.ppermute only.
A program may use at most 192 MiB of HBM per device.

```python
import math
import jax
import jax.numpy as jnp
import numpy as np
from jax import lax

ASKER_PLANES = 32
KV_HEADS = 4
HEAD_DIM = 128
ROT_DIM = 64
TOK_DEV = 128
DOCS = 16
SEQUENCE_SIZE = 4096
MAXDOC = 3072


def draw_decay_rate(key, part):
    matched_embeddings = jax.random.split(jax.random.fold_in(key, 3), 7)
    fast_share = 0.5
    fast = jax.random.uniform(matched_embeddings[0], (ASKER_PLANES, 1)) < fast_share
    fast_rate = jnp.exp(jax.random.uniform(matched_embeddings[1], (ASKER_PLANES, 1), minval=math.log(1.0 / 50.0), maxval=math.log(1.0 / 30.0)))
    slow_rate = jnp.exp(jax.random.uniform(matched_embeddings[2], (ASKER_PLANES, 1), minval=math.log(0.05), maxval=math.log(0.3))) / SEQUENCE_SIZE
    base_rate = jnp.where(fast, fast_rate, slow_rate)
    blocks = SEQUENCE_SIZE // TOK_DEV
    block_factor = jnp.exp(jax.random.uniform(matched_embeddings[3], (ASKER_PLANES, blocks, 1), minval=-0.7, maxval=0.7))
    token_factor = jnp.exp(jax.random.uniform(matched_embeddings[4], (ASKER_PLANES, blocks, TOK_DEV), minval=-0.3, maxval=0.3))
    forgetting_factors = (base_rate[:, :, None] * block_factor * token_factor).reshape(ASKER_PLANES, SEQUENCE_SIZE)
    segment_place = jax.random.randint(matched_embeddings[5], (ASKER_PLANES, 2), 0, SEQUENCE_SIZE)
    segment_extent = jax.random.uniform(matched_embeddings[6], (ASKER_PLANES, 2), minval=math.log(1.25), maxval=math.log(2.0))
    element_shift_number = jnp.arange(SEQUENCE_SIZE)[None, :]
    segment_ranges = jnp.where(element_shift_number == segment_place[:, 0:1], segment_extent[:, 0:1], 0.0) + jnp.where(element_shift_number == segment_place[:, 1:2], segment_extent[:, 1:2], 0.0)
    return (forgetting_factors + segment_ranges).astype(jnp.float32)


def base_values(key, shape):
    return jnp.clip(jax.random.normal(key, shape), -6.0, 6.0)


def draw_sm_key(key, part):
    base = base_values(jax.random.fold_in(key, 21), (SEQUENCE_SIZE, KV_HEADS, HEAD_DIM))
    return base.reshape(SEQUENCE_SIZE, KV_HEADS * HEAD_DIM).astype(jnp.float32)


def draw_sm_query(key, part):
    group = ASKER_PLANES // KV_HEADS
    base = base_values(jax.random.fold_in(key, 31), (SEQUENCE_SIZE, KV_HEADS, group, HEAD_DIM))
    return base.reshape(SEQUENCE_SIZE, ASKER_PLANES * HEAD_DIM).astype(jnp.float32)


def block_levels(rng, extent, cuts, smallest, high):
    gain = 1.0
    for position, parts in cuts:
        steps = jax.random.uniform(jax.random.fold_in(jax.random.fold_in(rng, 6), position), (parts,), jnp.float32, smallest / len(cuts), high / len(cuts))
        gain = gain * jnp.repeat(jnp.exp(steps), extent[position] // parts).reshape((-1,) + (1,) * (len(extent) - 1 - position))
    return gain


def length_profile(amount, total, most, lean):
    loads = [(1 << 20) // math.isqrt(standing ** lean) + 1 for standing in range(2, amount + 1)]
    spare, given = total - most - (amount - 1), [1] * (amount - 1)
    while spare > 0:
        candidates = [i for i in range(amount - 1) if given[i] < most]
        pool, left = sum([loads[i] for i in candidates]), spare
        for i in candidates:
            addition = min(most - given[i], max(1, left * loads[i] // pool), spare)
            given[i] = given[i] + addition
            spare = spare - addition
    return np.array([most] + given)


def uneven(key, count, total, bound, lean):
    if count == 2:
        one = jax.random.randint(key, (), max(1, total - bound), min(bound, total - 1) + 1)
        return jnp.stack([one, total - one])
    lengths = jnp.asarray(length_profile(count, total, bound, lean), jnp.int32)
    pairs = (count - 1) // 2
    giver, sink = lengths[1:1 + 2 * pairs:2], lengths[2:2 + 2 * pairs:2]
    room = jnp.minimum(giver - 1, bound - sink)
    shifted = jax.random.randint(jax.random.fold_in(key, 1), (pairs,), 0, 1 << 20) % (room + 1)
    lengths = lengths.at[1:1 + 2 * pairs:2].set(giver - shifted).at[2:2 + 2 * pairs:2].set(sink + shifted)
    return lengths[jax.random.permutation(jax.random.fold_in(key, 2), count)]


def scatter_about(stream_key, dims, scale, most, shards=(), kind=jnp.bfloat16):
    values = scale * jax.random.normal(stream_key, dims, jnp.float32)
    if shards:
        values = values * block_levels(stream_key, dims, shards, -0.22, 0.18)
    return jnp.clip(values, -most, most).astype(kind)


def setup_inputs(seed: int = 0, part: int = 0) -> dict:
    splits = jax.random.split(jax.random.key(seed), 11)
    part_splits = jax.random.split(jax.random.fold_in(splits[10], part), 11)
    return {
        "lin_query": scatter_about(part_splits[0], (SEQUENCE_SIZE, ASKER_PLANES * HEAD_DIM), 1.0, 6.0, ((0, 32), (1, 2)), jnp.float32),
        "lin_key": scatter_about(part_splits[1], (SEQUENCE_SIZE, ASKER_PLANES * HEAD_DIM), 1.0, 6.0, ((0, 32), (1, 2)), jnp.float32),
        "lin_value": scatter_about(part_splits[2], (SEQUENCE_SIZE, ASKER_PLANES * HEAD_DIM), 1.0, 6.0, ((0, 32), (1, 2)), jnp.float32),
        "lin_gate": scatter_about(part_splits[3], (SEQUENCE_SIZE, ASKER_PLANES * HEAD_DIM), 1.5, 8.0, ((0, 32), (1, 2)), jnp.float32),
        "decay_rate": draw_decay_rate(jax.random.fold_in(jax.random.fold_in(splits[10], part), 71), part),
        "norm_gain": jnp.clip(1.0 + 0.1 * jax.random.normal(splits[5], (ASKER_PLANES * HEAD_DIM,), jnp.float32), 0.5, 1.5),
        "sm_query": draw_sm_query(jax.random.fold_in(jax.random.fold_in(splits[10], part), 71), part),
        "sm_key": draw_sm_key(jax.random.fold_in(jax.random.fold_in(splits[10], part), 71), part),
        "sm_value": scatter_about(part_splits[8], (SEQUENCE_SIZE, KV_HEADS * HEAD_DIM), 1.0, 6.0, ((0, 32), (1, 2)), jnp.float32),
        "doc_lengths": uneven(part_splits[9], DOCS, SEQUENCE_SIZE, MAXDOC, 2).astype(jnp.int32),
    }


rope_base = 10000000.0
norm_eps = 1e-05
highest = lax.Precision.HIGHEST

def doc_tables(doc_lengths):
    doc_ends = jnp.cumsum(doc_lengths).astype(jnp.int32)
    doc_starts = (doc_ends - doc_lengths).astype(jnp.int32)
    return (doc_starts, doc_ends)

def doc_number(tokens_at, doc_ends):
    return lax.optimization_barrier(jnp.sum((doc_ends[None, :] <= tokens_at[:, None]).astype(jnp.int32), axis=1))

def doc_begin(tokens_at, doc_starts):
    picked = jnp.where(doc_starts[None, :] <= tokens_at[:, None], doc_starts[None, :], 0)
    return lax.optimization_barrier(jnp.max(picked, axis=1)).astype(jnp.int32)

def lightning_block(query_heads, key_heads, value_heads, forgetting_factors, first_token, doc_starts, doc_ends):
    width = query_heads.shape[1]
    tokens_at = first_token + jnp.arange(width, dtype=jnp.int32)
    doc_ids = doc_number(tokens_at, doc_ends)
    begins = doc_begin(tokens_at, doc_starts)
    log_decay = jnp.cumsum(-forgetting_factors, axis=1)
    visible = (doc_ids[:, None] == doc_ids[None, :]) & (tokens_at[:, None] >= tokens_at[None, :])
    spread = jnp.where(visible[None], log_decay[:, :, None] - log_decay[:, None, :], 0.0)
    weight = jnp.where(visible[None], jnp.exp(spread), 0.0)
    scores = jnp.einsum('htd,hsd->hts', query_heads, key_heads, precision=highest) * weight
    intra = jnp.einsum('hts,hsd->htd', scores, value_heads, precision=highest)
    carried_rows = begins < first_token
    block_decay = jnp.where(carried_rows[-1], jnp.exp(log_decay[:, -1]), 0.0)
    in_tail = doc_ids == doc_ids[-1]
    tail_gap = jnp.where(in_tail[None], log_decay[:, -1:] - log_decay, 0.0)
    tail_weight = jnp.where(in_tail[None], jnp.exp(tail_gap), 0.0)
    block_inner = jnp.einsum('htd,hte->hde', key_heads * tail_weight[:, :, None], value_heads, precision=highest)
    return (intra, log_decay, carried_rows, block_decay, block_inner)

def carried_term(query_heads, state, log_decay, carried_rows):
    reach_weight = jnp.where(carried_rows[None], jnp.exp(log_decay), 0.0)
    return jnp.einsum('htd,hde->hte', query_heads, state, precision=highest) * reach_weight[:, :, None]

def finish(attention, lin_gate, norm_gain):
    rows_count = attention.shape[0]
    per_head = attention.reshape(rows_count, -1, HEAD_DIM)
    mean_square = lax.optimization_barrier(jnp.mean(per_head * per_head, axis=-1, keepdims=True))
    normed = (per_head / jnp.sqrt(mean_square + norm_eps)).reshape(rows_count, -1)
    return normed * norm_gain[None, :] * jax.nn.sigmoid(lin_gate)

def rotate(heads_in, positions):
    half = ROT_DIM // 2
    inverse = rope_base ** (-(2.0 * jnp.arange(half, dtype=jnp.float32)) / ROT_DIM)
    angle = positions.astype(jnp.float32)[:, None] * inverse[None, :]
    cosine = jnp.cos(angle)[:, None, :]
    sine = jnp.sin(angle)[:, None, :]
    first_half = heads_in[..., :half]
    second_half = heads_in[..., half:ROT_DIM]
    return jnp.concatenate([first_half * cosine - second_half * sine, second_half * cosine + first_half * sine, heads_in[..., ROT_DIM:]], axis=-1)

def lightning(lin_query, lin_key, lin_value, decay_rate, doc_starts, doc_ends):
    blocks = SEQUENCE_SIZE // TOK_DEV

    def split_heads(matrix):
        return matrix.reshape(blocks, TOK_DEV, ASKER_PLANES, HEAD_DIM).transpose(0, 2, 1, 3)
    forgetting_factors = decay_rate.reshape(ASKER_PLANES, blocks, TOK_DEV).transpose(1, 0, 2)
    firsts = (jnp.arange(blocks, dtype=jnp.int32) * TOK_DEV).astype(jnp.int32)

    def advance(state, pieces):
        query_block, key_block, value_block, rate_block, first_token = pieces
        intra, log_decay, carried_rows, block_decay, block_inner = lightning_block(query_block, key_block, value_block, rate_block, first_token, doc_starts, doc_ends)
        result = intra + carried_term(query_block, state, log_decay, carried_rows)
        state = block_decay[:, None, None] * state + block_inner
        return (state, result)
    initial = jnp.zeros((ASKER_PLANES, HEAD_DIM, HEAD_DIM), jnp.float32)
    _, outputs = lax.scan(advance, initial, (split_heads(lin_query), split_heads(lin_key), split_heads(lin_value), forgetting_factors, firsts))
    return outputs.transpose(0, 2, 1, 3).reshape(SEQUENCE_SIZE, ASKER_PLANES * HEAD_DIM)

def softmax_layer(sm_query, sm_key, sm_value, doc_starts, doc_ends):
    group = ASKER_PLANES // KV_HEADS
    tokens_at = jnp.arange(SEQUENCE_SIZE, dtype=jnp.int32)
    positions = tokens_at - doc_begin(tokens_at, doc_starts)
    doc_ids = doc_number(tokens_at, doc_ends)
    queries = rotate(sm_query.reshape(SEQUENCE_SIZE, ASKER_PLANES, HEAD_DIM), positions)
    keys_all = rotate(sm_key.reshape(SEQUENCE_SIZE, KV_HEADS, HEAD_DIM), positions)
    values_all = sm_value.reshape(SEQUENCE_SIZE, KV_HEADS, HEAD_DIM)
    scale = HEAD_DIM ** (-0.5)
    blocks = SEQUENCE_SIZE // TOK_DEV

    def one_block(index):
        first_token = (index * TOK_DEV).astype(jnp.int32)
        query_rows = lax.dynamic_slice_in_dim(queries, first_token, TOK_DEV, 0).reshape(TOK_DEV, KV_HEADS, group, HEAD_DIM)
        rows_at = first_token + jnp.arange(TOK_DEV, dtype=jnp.int32)
        row_docs = lax.dynamic_slice_in_dim(doc_ids, first_token, TOK_DEV, 0)
        visible = (row_docs[:, None] == doc_ids[None, :]) & (rows_at[:, None] >= tokens_at[None, :])
        scores = jnp.einsum('tkgd,skd->kgts', query_rows, keys_all, precision=highest) * scale
        masked = jnp.where(visible[None, None], scores, -jnp.inf)
        top = lax.optimization_barrier(jnp.max(masked, axis=-1, keepdims=True))
        weights = jnp.where(visible[None, None], jnp.exp(masked - top), 0.0)
        total = lax.optimization_barrier(jnp.sum(weights, axis=-1))
        mixed = jnp.einsum('kgts,skd->kgtd', weights, values_all, precision=highest) / total[..., None]
        return mixed.transpose(2, 0, 1, 3).reshape(TOK_DEV, ASKER_PLANES * HEAD_DIM)
    outputs = lax.map(one_block, jnp.arange(blocks, dtype=jnp.int32))
    return outputs.reshape(SEQUENCE_SIZE, ASKER_PLANES * HEAD_DIM)

def reference(lin_query, lin_key, lin_value, lin_gate, decay_rate, norm_gain, sm_query, sm_key, sm_value, doc_lengths):
    doc_starts, doc_ends = doc_tables(doc_lengths)
    attention = lightning(lin_query, lin_key, lin_value, decay_rate, doc_starts, doc_ends)
    lin_out = finish(attention, lin_gate, norm_gain)
    sm_out = softmax_layer(sm_query, sm_key, sm_value, doc_starts, doc_ends)
    return (lin_out, sm_out)
```

```python
import functools
import math

import jax
import jax.numpy as jnp
import numpy as np
from jax import lax
from jax.experimental import pallas as pl
from jax.experimental.pallas import tpu as pltpu
from jax.sharding import Mesh, PartitionSpec as P

HEAD_DIM = 128
ROT_DIM = 64
TOK = 128
DOCS = 16
CHUNK = 512
NEG = -1e30
ROPE_BASE = 10000000.0
NORM_EPS = 1e-05
F32 = jnp.float32
BF16 = jnp.bfloat16

INVERSE = np.power(
    ROPE_BASE, -(2.0 * np.arange(ROT_DIM // 2, dtype=np.float64)) / ROT_DIM
).astype(np.float32)

SMEM = pl.BlockSpec(memory_space=pltpu.SMEM)


def built(kernel, out_shape, shapes, scratch=(), flops=1_000_000, moved=1_000_000, limit=20):
    def whole(shape):
        return pl.BlockSpec(shape, lambda i: (0,) * len(shape))

    many = isinstance(out_shape, (tuple, list))
    return pl.pallas_call(
        kernel,
        out_shape=out_shape,
        grid=(1,),
        in_specs=[SMEM] + [whole(shape) for shape in shapes],
        out_specs=[whole(o.shape) for o in out_shape] if many else whole(out_shape.shape),
        scratch_shapes=list(scratch),
        compiler_params=pltpu.CompilerParams(vmem_limit_bytes=limit << 20),
        cost_estimate=pl.CostEstimate(
            flops=flops, bytes_accessed=moved, transcendentals=0
        ),
    )


def call(kernel, out_shape, n_in, **options):
    def run(lengths, *arrays):
        return built(kernel, out_shape, [a.shape for a in arrays], **options)(lengths, *arrays)

    return run


def halves(x):
    high = x.astype(BF16)
    return high, (x - high.astype(F32)).astype(BF16)


def dot(a, b, ca, cb):
    return lax.dot_general(a, b, (((ca,), (cb,)), ((), ())), preferred_element_type=F32)


def dot3(a, b, ca, cb):
    ah, al = halves(a)
    bh, bl = halves(b)
    return dot(ah, bh, ca, cb) + (dot(ah, bl, ca, cb) + dot(al, bh, ca, cb))


def begins_of(lengths_ref, tokens):
    begin = jnp.zeros_like(tokens)
    start = jnp.int32(0)
    for d in range(DOCS - 1):
        start = start + lengths_ref[d]
        begin = jnp.where(tokens >= start, start, begin)
    return begin


def begin_scalar(lengths_ref, token):
    begin = jnp.int32(0)
    start = jnp.int32(0)
    for d in range(DOCS - 1):
        start = start + lengths_ref[d]
        begin = jnp.where(token >= start, start, begin)
    return begin


def block_of():
    return lax.axis_index("y") * lax.axis_size("z") + lax.axis_index("z")


def rope_tables(lengths_ref, inverse_ref, first):
    rows = first + lax.broadcasted_iota(jnp.int32, (TOK, HEAD_DIM), 0)
    lane = lax.broadcasted_iota(jnp.int32, (TOK, HEAD_DIM), 1)
    position = (rows - begins_of(lengths_ref, rows)).astype(F32)
    angle = position * inverse_ref[...]
    rotated = lane < ROT_DIM
    cosine = jnp.where(rotated, jnp.cos(angle), 1.0)
    sine = jnp.sin(angle)
    low = jnp.where(lane < ROT_DIM // 2, -sine, 0.0)
    high = jnp.where(rotated & (lane >= ROT_DIM // 2), sine, 0.0)
    return cosine, low, high


def rotated(x, tables):
    cosine, low, high = tables
    half = ROT_DIM // 2
    return (
        x * cosine
        + pltpu.roll(x, HEAD_DIM - half, 1) * low
        + pltpu.roll(x, half, 1) * high
    )


def kv_kernel(lengths_ref, inverse_ref, key_ref, value_ref, tables_ref, *pieces):
    tables = rope_tables(lengths_ref, inverse_ref, block_of() * TOK)
    for i in range(3):
        tables_ref[i] = tables[i]
    mine = lax.axis_index("y")
    for a in range(2):
        lanes = slice(a * HEAD_DIM, (a + 1) * HEAD_DIM)
        k = rotated(key_ref[:, lanes], tables)
        v = value_ref[:, lanes]
        for r in range(4):
            for b, x in ((0, k), (1, v)):

                @pl.when((mine + r) % 4 == 2 * a + b)
                def _():
                    pieces[r][...] = x


def query_kernel(lengths_ref, tables_ref, query_ref, *pieces):
    tables = [tables_ref[i] for i in range(3)]
    mine = lax.axis_index("y")
    scale = math.log2(math.e) / math.sqrt(HEAD_DIM)
    for r in range(4):
        e = (mine + r) % 4
        for n in range(4):
            at = pl.multiple_of(e * (4 * HEAD_DIM) + n * HEAD_DIM, HEAD_DIM)
            x = query_ref[:, pl.ds(at, HEAD_DIM)]
            pieces[r][:, n * HEAD_DIM : (n + 1) * HEAD_DIM] = rotated(x, tables) * scale


def softmax_kernel(lengths_ref, *refs):
    queries, kv_ref, outs = refs[:4], refs[4], refs[5:9]
    kcat, vcat, qcat, s_ref, m_ref, l_ref, acc_ref = refs[9:]
    z = lax.axis_index("z")
    zs = kv_ref.shape[0]
    e_key = 2 * (lax.axis_index("y") % 2)
    e = e_key + lax.axis_index("head")
    last = 3 * zs + z

    @pl.loop(0, last + 1)
    def _(b):
        at = pl.multiple_of(b * TOK, TOK)
        kh, kl = halves(kv_ref[b % zs, 0, (e_key - b // zs + 4) % 4])
        vh, vl = halves(kv_ref[b % zs, 1, (e_key + 1 - b // zs + 4) % 4])
        kcat[pl.ds(at, TOK), 0:128] = kh
        kcat[pl.ds(at, TOK), 128:256] = kh
        kcat[pl.ds(at, TOK), 256:384] = kl
        vcat[pl.ds(at, TOK), 0:128] = vh
        vcat[pl.ds(at, TOK), 128:256] = vl

    @pl.loop(last + 1, 4 * zs)
    def _(b):
        at = pl.multiple_of(b * TOK, TOK)
        kcat[pl.ds(at, TOK), :] = jnp.zeros((TOK, 384), BF16)
        vcat[pl.ds(at, TOK), :] = jnp.zeros((TOK, 256), BF16)

    for r in range(4):
        block = ((e - r + 4) % 4) * zs + z
        first = block * TOK
        rows = first + lax.broadcasted_iota(jnp.int32, (TOK, CHUNK), 0)
        begin = begins_of(lengths_ref, rows)
        for n in range(4):
            qh, ql = halves(queries[r][:, n * HEAD_DIM : (n + 1) * HEAD_DIM])
            qcat[n * TOK : (n + 1) * TOK, 0:128] = qh
            qcat[n * TOK : (n + 1) * TOK, 128:256] = ql
            qcat[n * TOK : (n + 1) * TOK, 256:384] = qh
        low = begin_scalar(lengths_ref, first) // CHUNK
        high = first // CHUNK + 1
        inner = (begin_scalar(lengths_ref, first + TOK - 1) + CHUNK - 1) // CHUNK
        inner = jnp.minimum(inner, high)
        outer = jnp.maximum(inner, high - 1)
        m_ref[...] = jnp.full_like(m_ref, NEG)
        l_ref[...] = jnp.zeros_like(l_ref)
        acc_ref[...] = jnp.zeros_like(acc_ref)

        def score(j, masked):
            at = pl.multiple_of(j * CHUNK, CHUNK)
            s = dot(qcat[...], kcat[pl.ds(at, CHUNK), :], 1, 1)
            if masked:
                keys = at + lax.broadcasted_iota(jnp.int32, (TOK, CHUNK), 1)
                visible = (keys >= begin) & (keys <= rows)
                s = jnp.where(visible[None], s.reshape(4, TOK, CHUNK), NEG)
                s = s.reshape(4 * TOK, CHUNK)
            s_ref[j] = s
            top = s[:, :HEAD_DIM]
            for i in range(1, CHUNK // HEAD_DIM):
                top = jnp.maximum(top, s[:, i * HEAD_DIM : (i + 1) * HEAD_DIM])
            m_ref[...] = jnp.maximum(m_ref[...], top)

        pl.loop(low, inner)(lambda j: score(j, True))
        pl.loop(inner, outer)(lambda j: score(j, False))
        pl.loop(outer, high)(lambda j: score(j, True))

        top = jnp.max(m_ref[...], axis=1, keepdims=True)
        m_ref[...] = jnp.broadcast_to(top, m_ref.shape)

        @pl.loop(low, high)
        def _(j):
            at = pl.multiple_of(j * CHUNK, CHUNK)
            top = m_ref[...]
            highs, lows, total = [], [], l_ref[...]
            for i in range(CHUNK // HEAD_DIM):
                p = jnp.exp2(s_ref[j, :, i * HEAD_DIM : (i + 1) * HEAD_DIM] - top)
                total = total + p
                ph, pl_ = halves(p)
                highs.append(ph)
                lows.append(pl_)
            l_ref[...] = total
            v = vcat[pl.ds(at, CHUNK), :]
            p = jnp.concatenate(highs + lows, axis=1)
            acc_ref[...] += dot(p, jnp.concatenate([v, v], axis=0), 1, 0)

        total = jnp.sum(l_ref[...], axis=1, keepdims=True)
        mixed = (acc_ref[:, :HEAD_DIM] + acc_ref[:, HEAD_DIM:]) / total
        for n in range(4):
            outs[r][:, n * HEAD_DIM : (n + 1) * HEAD_DIM] = mixed[n * TOK : (n + 1) * TOK]


def place_kernel(lengths_ref, *refs):
    pieces, out_ref = refs[:4], refs[4]
    mine = lax.axis_index("y")
    width = 4 * HEAD_DIM
    for r in range(4):
        at = pl.multiple_of(((mine + r) % 4) * width, width)
        out_ref[:, pl.ds(at, width)] = pieces[r][...]


def thirds(x):
    high = x.astype(BF16)
    rest = x - high.astype(F32)
    mid = rest.astype(BF16)
    return high, mid, (rest - mid.astype(F32)).astype(BF16)


def dot6(a, b, ca, cb):
    ah, am, al = thirds(a)
    bh, bm, bl = thirds(b)
    small = dot(ah, bl, ca, cb) + dot(al, bh, ca, cb) + dot(am, bm, ca, cb)
    return dot(ah, bh, ca, cb) + (dot(ah, bm, ca, cb) + dot(am, bh, ca, cb) + small)


def decay_columns(rate_ref):
    t = lax.broadcasted_iota(jnp.int32, (TOK, TOK), 0)
    s = lax.broadcasted_iota(jnp.int32, (TOK, TOK), 1)
    lower = jnp.where(s <= t, 1.0, 0.0).astype(BF16)
    parts = [dot(lower, x, 1, 1) for x in thirds(-rate_ref[...])]
    return parts[0] + (parts[1] + parts[2])


def decay_rows(rate_ref):
    s = lax.broadcasted_iota(jnp.int32, (TOK, TOK), 0)
    t = lax.broadcasted_iota(jnp.int32, (TOK, TOK), 1)
    upper = jnp.where(s <= t, 1.0, 0.0).astype(BF16)
    parts = [dot(x, upper, 1, 0) for x in thirds(-rate_ref[...])]
    return parts[0] + (parts[1] + parts[2])


def state_kernel(lengths_ref, rate_ref, key_ref, value_ref, out_ref):
    heads = rate_ref.shape[0]
    first = block_of() * TOK
    tail = begin_scalar(lengths_ref, first + TOK - 1)
    columns = decay_columns(rate_ref)
    rows = first + lax.broadcasted_iota(jnp.int32, (TOK, heads), 0)
    end = columns[TOK - 1 : TOK, :]
    weight = jnp.where(
        rows >= tail, jnp.exp(jnp.where(rows >= tail, end - columns, 0.0)), 0.0
    )
    carried = jnp.where(tail < first, jnp.exp(end), 0.0)
    half = HEAD_DIM // 2
    for h in range(heads):
        lanes = slice(h * HEAD_DIM, (h + 1) * HEAD_DIM)
        k = key_ref[:, lanes] * weight[:, h : h + 1]
        inner = dot3(k, value_ref[:, lanes], 0, 0)
        kept = jnp.broadcast_to(carried[:, h : h + 1], (8, HEAD_DIM))
        for i in range(2):
            out_ref[2 * h + i, :half] = inner[i * half : (i + 1) * half]
            out_ref[2 * h + i, half:] = kept


def prefix_kernel(lengths_ref, in_ref, out_ref):
    blocks, half = out_ref.shape[0], out_ref.shape[1]
    state = jnp.zeros(out_ref.shape[1:], F32)
    for i in range(blocks):
        out_ref[i] = state
        if i < blocks - 1:
            state = in_ref[i, half : half + 1, :] * state + in_ref[i, :half, :]


def intra_kernel(lengths_ref, rate_ref, query_ref, key_ref, value_ref, out_ref):
    heads = rate_ref.shape[0]
    first = block_of() * TOK
    columns = decay_columns(rate_ref)
    across = decay_rows(rate_ref)
    t = first + lax.broadcasted_iota(jnp.int32, (TOK, TOK), 0)
    s = first + lax.broadcasted_iota(jnp.int32, (TOK, TOK), 1)
    visible = (s <= t) & (s >= begins_of(lengths_ref, t))
    for h in range(heads):
        lanes = slice(h * HEAD_DIM, (h + 1) * HEAD_DIM)
        gap = jnp.where(visible, columns[:, h : h + 1] - across[h : h + 1, :], 0.0)
        weight = jnp.where(visible, jnp.exp(gap), 0.0)
        scores = dot6(query_ref[:, lanes], key_ref[:, lanes], 1, 1) * weight
        out_ref[:, lanes] = dot3(scores, value_ref[:, lanes], 1, 0)


def finish_kernel(
    lengths_ref, rate_ref, query_ref, state_ref, intra_ref, gate_ref, gain_ref, out_ref
):
    heads = rate_ref.shape[0]
    first = block_of() * TOK
    columns = decay_columns(rate_ref)
    rows = first + lax.broadcasted_iota(jnp.int32, (TOK, heads), 0)
    carried = begins_of(lengths_ref, rows) < first
    reach = jnp.where(carried, jnp.exp(columns), 0.0)
    for h in range(heads):
        lanes = slice(h * HEAD_DIM, (h + 1) * HEAD_DIM)
        x = intra_ref[:, lanes] + dot3(query_ref[:, lanes], state_ref[h], 1, 0) * reach[
            :, h : h + 1
        ]
        mean = jnp.mean(x * x, axis=1, keepdims=True)
        normed = x / jnp.sqrt(mean + NORM_EPS)
        gate = 1.0 / (1.0 + jnp.exp(-gate_ref[:, lanes]))
        out_ref[:, lanes] = normed * gain_ref[:, lanes] * gate


def shards(
    lin_query,
    lin_key,
    lin_value,
    lin_gate,
    decay_rate,
    norm_gain,
    sm_query,
    sm_key,
    sm_value,
    doc_lengths,
):
    rows, width = lin_query.shape
    heads = width // HEAD_DIM
    ys, zs = lax.axis_size("y"), lax.axis_size("z")
    blocks = ys * zs
    group = ("y", "head")
    out = jax.ShapeDtypeStruct
    forth, back = [], []
    for r in range(4):
        pairs = []
        for y in range(ys):
            for h in range(2):
                piece = (y + r) % 4
                pairs.append((2 * y + h, 2 * (2 * h + piece // 2) + piece % 2))
        forth.append(pairs)
        back.append([(b, a) for a, b in pairs])

    inverse = np.zeros((1, HEAD_DIM), np.float32)
    inverse[0, :ROT_DIM] = np.tile(INVERSE, 2)
    tables, *kv_pieces = call(
        kv_kernel,
        [out((3, rows, HEAD_DIM), F32)] + [out((rows, HEAD_DIM), F32)] * 4,
        4,
        moved=800_000,
        limit=60,
    )(doc_lengths, jnp.asarray(inverse), sm_key, sm_value)
    kv_here = [lax.ppermute(p, group, forth[r]) for r, p in enumerate(kv_pieces)]
    kv = lax.all_gather(jnp.stack(kv_here), ("z", "head"), axis=0, tiled=False)
    kv = kv.reshape(zs, 2, ys, rows, HEAD_DIM)

    sliced = call(
        state_kernel,
        out((blocks, HEAD_DIM // 2 + 8, HEAD_DIM), F32),
        4,
        flops=6 * heads * HEAD_DIM**3,
        moved=3_300_000,
        limit=60,
    )(doc_lengths, decay_rate, lin_key, lin_value)
    arrived = lax.all_to_all(sliced, ("y", "z"), 0, 0, tiled=True)

    q_pieces = call(
        query_kernel, [out((rows, 4 * HEAD_DIM), F32)] * 4, 3, moved=2_200_000
    )(doc_lengths, tables, sm_query)
    queries = [lax.ppermute(p, group, forth[r]) for r, p in enumerate(q_pieces)]

    intra = call(
        intra_kernel,
        out((rows, width), F32),
        5,
        flops=12 * heads * HEAD_DIM**3,
        moved=4_200_000,
    )(doc_lengths, decay_rate, lin_query, lin_key, lin_value)

    arrived, intra, *queries = lax.optimization_barrier((arrived, intra, *queries))
    prefixes = call(
        prefix_kernel, out((blocks, HEAD_DIM // 2, HEAD_DIM), F32), 2, moved=2_200_000
    )(doc_lengths, arrived)
    state = lax.all_to_all(prefixes, ("y", "z"), 0, 0, tiled=True)
    state = state.reshape(heads, HEAD_DIM, HEAD_DIM)

    mixed = call(
        softmax_kernel,
        [out((rows, 4 * HEAD_DIM), F32)] * 4,
        6,
        scratch=[
            pltpu.VMEM((blocks * TOK, 384), BF16),
            pltpu.VMEM((blocks * TOK, 256), BF16),
            pltpu.VMEM((4 * TOK, 384), BF16),
            pltpu.VMEM((blocks * TOK // CHUNK, 4 * TOK, CHUNK), F32),
            pltpu.VMEM((4 * TOK, HEAD_DIM), F32),
            pltpu.VMEM((4 * TOK, HEAD_DIM), F32),
            pltpu.VMEM((4 * TOK, 2 * HEAD_DIM), F32),
        ],
        limit=32,
        flops=6 * 50 * 4 * 2 * 128**3,
        moved=6_000_000,
    )(doc_lengths, *queries, kv)
    returned = [lax.ppermute(p, group, back[r]) for r, p in enumerate(mixed)]

    lin_out = call(
        finish_kernel,
        out((rows, width), F32),
        7,
        flops=6 * heads * HEAD_DIM**3,
        moved=5_200_000,
    )(doc_lengths, decay_rate, lin_query, state, intra, lin_gate, norm_gain.reshape(1, width))
    sm_out = call(place_kernel, out((rows, width), F32), 5, moved=2_000_000)(
        doc_lengths, *returned
    )
    return (lin_out, sm_out)


def solution(mesh):
    sizes = mesh.shape
    ring = 4
    inner = Mesh(
        mesh.devices.reshape(ring, sizes["context"] // ring, sizes["head"], sizes["dp"]),
        ("y", "z", "head", "dp"),
    )
    tokens = ("dp", "y", "z")
    wide = P(tokens, "head")
    in_specs = (
        wide,
        wide,
        wide,
        wide,
        P("head", tokens),
        P("head"),
        wide,
        wide,
        wide,
        P("dp"),
    )
    return jax.shard_map(
        shards, mesh=inner, in_specs=in_specs, out_specs=(wide, wide), check_vma=False
    )
```

```python
import functools
import math

import jax
import jax.numpy as jnp
import numpy as np
from jax import lax
from jax.experimental import pallas as pl
from jax.experimental.pallas import tpu as pltpu
from jax.sharding import Mesh, PartitionSpec as P

HEAD_DIM = 128
ROT_DIM = 64
TOK = 128
DOCS = 16
CHUNK = 512
PIECES = (0, 1, -1, 2, -2, 3, -3, 4)
NEG = -1e30
QUERIES = 4 * HEAD_DIM
ROPE_BASE = 10000000.0
NORM_EPS = 1e-05
F32 = jnp.float32
BF16 = jnp.bfloat16

INVERSE = np.power(
    ROPE_BASE, -(2.0 * np.arange(ROT_DIM // 2, dtype=np.float64)) / ROT_DIM
).astype(np.float32)

VMEM = pl.BlockSpec(memory_space=pltpu.VMEM)
SMEM = pl.BlockSpec(memory_space=pltpu.SMEM)


def built(kernel, out_shape, shapes, scratch=(), flops=1000, moved=1000, limit=20):
    def whole(shape):
        return pl.BlockSpec(shape, lambda i: (0,) * len(shape))

    many = isinstance(out_shape, (tuple, list))
    return pl.pallas_call(
        kernel,
        out_shape=out_shape,
        grid=(1,),
        in_specs=[SMEM] + [whole(shape) for shape in shapes],
        out_specs=[whole(o.shape) for o in out_shape] if many else whole(out_shape.shape),
        scratch_shapes=list(scratch),
        compiler_params=pltpu.CompilerParams(vmem_limit_bytes=limit << 20),
        cost_estimate=pl.CostEstimate(
            flops=flops, bytes_accessed=moved, transcendentals=0
        ),
    )


def call(kernel, out_shape, n_in, **options):
    def run(lengths, *arrays):
        return built(kernel, out_shape, [a.shape for a in arrays], **options)(lengths, *arrays)

    return run


def halves(x):
    high = x.astype(BF16)
    return high, (x - high.astype(F32)).astype(BF16)


def dot(a, b, ca, cb):
    return lax.dot_general(a, b, (((ca,), (cb,)), ((), ())), preferred_element_type=F32)


def dot3(a, b, ca, cb):
    ah, al = halves(a)
    bh, bl = halves(b)
    return dot(ah, bh, ca, cb) + (dot(ah, bl, ca, cb) + dot(al, bh, ca, cb))


def begins_of(lengths_ref, tokens):
    begin = jnp.zeros_like(tokens)
    start = jnp.int32(0)
    for d in range(DOCS - 1):
        start = start + lengths_ref[d]
        begin = jnp.where(tokens >= start, start, begin)
    return begin


def begin_scalar(lengths_ref, token):
    begin = jnp.int32(0)
    start = jnp.int32(0)
    for d in range(DOCS - 1):
        start = start + lengths_ref[d]
        begin = jnp.where(token >= start, start, begin)
    return begin


def block_of():
    return lax.axis_index("y") * lax.axis_size("z") + lax.axis_index("z")


def rope_tables(lengths_ref, inverse_ref, first):
    rows = first + lax.broadcasted_iota(jnp.int32, (TOK, HEAD_DIM), 0)
    lane = lax.broadcasted_iota(jnp.int32, (TOK, HEAD_DIM), 1)
    position = (rows - begins_of(lengths_ref, rows)).astype(F32)
    angle = position * inverse_ref[...]
    rotated = lane < ROT_DIM
    cosine = jnp.where(rotated, jnp.cos(angle), 1.0)
    sine = jnp.sin(angle)
    low = jnp.where(lane < ROT_DIM // 2, -sine, 0.0)
    high = jnp.where(rotated & (lane >= ROT_DIM // 2), sine, 0.0)
    return cosine, low, high


def rotated(x, tables):
    cosine, low, high = tables
    half = ROT_DIM // 2
    return (
        x * cosine
        + pltpu.roll(x, HEAD_DIM - half, 1) * low
        + pltpu.roll(x, half, 1) * high
    )


def kv_kernel(lengths_ref, inverse_ref, key_ref, value_ref, tables_ref, *pieces):
    tables = rope_tables(lengths_ref, inverse_ref, block_of() * TOK)
    for i in range(3):
        tables_ref[i] = tables[i]
    mine = lax.axis_index("y")
    for a in range(2):
        lanes = slice(a * HEAD_DIM, (a + 1) * HEAD_DIM)
        k = rotated(key_ref[:, lanes], tables)
        v = value_ref[:, lanes]
        for r in range(4):
            for b, x in ((0, k), (1, v)):

                @pl.when((mine + r) % 4 == 2 * a + b)
                def _():
                    pieces[r][...] = x


def query_kernel(lengths_ref, tables_ref, query_ref, *pieces):
    tables = [tables_ref[i] for i in range(3)]
    mine = lax.axis_index("y")
    scale = math.log2(math.e) / math.sqrt(HEAD_DIM)
    for r in range(4):
        e = (mine + r) % 4
        for n in range(4):
            at = pl.multiple_of(e * (4 * HEAD_DIM) + n * HEAD_DIM, HEAD_DIM)
            x = query_ref[:, pl.ds(at, HEAD_DIM)]
            pieces[r][:, n * HEAD_DIM : (n + 1) * HEAD_DIM] = rotated(x, tables) * scale


def pack(mine, theirs, kcat, vcat):
    z, zs = lax.axis_index("z"), lax.axis_size("z")
    core = lax.axis_index("head")
    e_key = 2 * (lax.axis_index("y") % 2)

    def keep(x, at, keys):
        high, low = halves(x)
        if keys:
            kcat[pl.ds(at, TOK), 0:128] = high
            kcat[pl.ds(at, TOK), 128:256] = high
            kcat[pl.ds(at, TOK), 256:384] = low
        else:
            vcat[pl.ds(at, TOK), 0:128] = high
            vcat[pl.ds(at, TOK), 128:256] = low

    def fill(i, own, keys):
        source = (z - PIECES[i] + zs) % zs

        @pl.loop(0, 4)
        def _(r):
            row = (e_key + (0 if keys else 1) - r + 4) % 4
            at = pl.multiple_of((row * zs + source) * TOK, TOK)
            if own:
                x = mine[i][r]
            elif i < 7:
                x = theirs[0][i, r]
            else:
                x = theirs[1][r]
            keep(x, at, keys)

    @pl.when(core == 0)
    def _():
        for i in range(8):
            fill(i, True, True)
            fill(i, False, False)

    @pl.when(core == 1)
    def _():
        for i in range(8):
            fill(i, True, False)
            fill(i, False, True)


def in_pairs(low, high, step):
    pairs = (high - low) // 2

    @pl.loop(0, pairs)
    def _(i):
        step(low + 2 * i)
        step(low + 2 * i + 1)

    pl.when((high - low) % 2 == 1)(lambda: step(high - 1))


def softmax_kernel(lengths_ref, *refs):
    queries, mine, theirs, outs = refs[:4], refs[4:12], refs[12:14], refs[14:18]
    kcat, vcat = refs[18:20]
    pack(mine, theirs, kcat, vcat)
    for r in range(4):
        attend(r, lengths_ref, queries[r], kcat, vcat, outs[r], *refs[20:])


def attend(r, lengths_ref, query_ref, kcat, vcat, out_ref, *scratch):
    qcat, s_ref, m_ref, l_ref, acc_ref = scratch
    e = 2 * (lax.axis_index("y") % 2) + lax.axis_index("head")
    block = ((e - r + 4) % 4) * lax.axis_size("z") + lax.axis_index("z")
    first = block * TOK
    for n in range(4):
        qh, ql = halves(query_ref[:, n * HEAD_DIM : (n + 1) * HEAD_DIM])
        qcat[n * TOK : (n + 1) * TOK, 0:128] = qh
        qcat[n * TOK : (n + 1) * TOK, 128:256] = ql
        qcat[n * TOK : (n + 1) * TOK, 256:384] = qh
    low = begin_scalar(lengths_ref, first) // CHUNK
    high = first // CHUNK + 1
    inner = (begin_scalar(lengths_ref, first + TOK - 1) + CHUNK - 1) // CHUNK
    inner = jnp.minimum(inner, high)
    outer = jnp.maximum(inner, high - 1)
    m_ref[...] = jnp.full_like(m_ref, NEG)
    l_ref[...] = jnp.zeros_like(l_ref)
    acc_ref[...] = jnp.zeros_like(acc_ref)

    def score(j, masked):
        at = pl.multiple_of(j * CHUNK, CHUNK)
        s = dot(qcat[...], kcat[pl.ds(at, CHUNK), :], 1, 1)
        if masked:
            rows = first + lax.broadcasted_iota(jnp.int32, (TOK, CHUNK), 0)
            keys = at + lax.broadcasted_iota(jnp.int32, (TOK, CHUNK), 1)
            begin = begins_of(
                lengths_ref, first + lax.broadcasted_iota(jnp.int32, (TOK, 1), 0)
            )
            visible = (keys >= begin) & (keys <= rows)
            s = jnp.where(visible[None], s.reshape(4, TOK, CHUNK), NEG)
            s = s.reshape(4 * TOK, CHUNK)
        s_ref[j] = s
        top = s[:, :HEAD_DIM]
        for i in range(1, CHUNK // HEAD_DIM):
            top = jnp.maximum(top, s[:, i * HEAD_DIM : (i + 1) * HEAD_DIM])
        m_ref[...] = jnp.maximum(m_ref[...], top)

    pl.loop(low, inner)(lambda j: score(j, True))
    in_pairs(inner, outer, lambda j: score(j, False))
    pl.loop(outer, high)(lambda j: score(j, True))

    top = jnp.max(m_ref[...], axis=1, keepdims=True)
    m_ref[...] = jnp.broadcast_to(top, m_ref.shape)

    def mix(j):
        at = pl.multiple_of(j * CHUNK, CHUNK)
        top = m_ref[...]
        highs, lows, total = [], [], l_ref[...]
        for i in range(CHUNK // HEAD_DIM):
            p = jnp.exp2(s_ref[j, :, i * HEAD_DIM : (i + 1) * HEAD_DIM] - top)
            total = total + p
            ph, pl_ = halves(p)
            highs.append(ph)
            lows.append(pl_)
        l_ref[...] = total
        v = vcat[pl.ds(at, CHUNK), :]
        p = jnp.concatenate(highs + lows, axis=1)
        acc_ref[...] += dot(p, jnp.concatenate([v, v], axis=0), 1, 0)

    in_pairs(low, high, mix)

    total = jnp.sum(l_ref[...], axis=1, keepdims=True)
    mixed = (acc_ref[:, :HEAD_DIM] + acc_ref[:, HEAD_DIM:]) / total
    for n in range(4):
        out_ref[:, n * HEAD_DIM : (n + 1) * HEAD_DIM] = mixed[n * TOK : (n + 1) * TOK]


def place_kernel(lengths_ref, *refs):
    pieces, out_ref = refs[:4], refs[4]
    mine = lax.axis_index("y")
    width = 4 * HEAD_DIM
    for r in range(4):
        at = pl.multiple_of(((mine + r) % 4) * width, width)
        out_ref[:, pl.ds(at, width)] = pieces[r][...]


def thirds(x):
    high = x.astype(BF16)
    rest = x - high.astype(F32)
    mid = rest.astype(BF16)
    return high, mid, (rest - mid.astype(F32)).astype(BF16)


def dot6(a, b, ca, cb):
    ah, am, al = thirds(a)
    bh, bm, bl = thirds(b)
    small = dot(ah, bl, ca, cb) + dot(al, bh, ca, cb) + dot(am, bm, ca, cb)
    return dot(ah, bh, ca, cb) + (dot(ah, bm, ca, cb) + dot(am, bh, ca, cb) + small)


def decay_columns(rate_ref):
    t = lax.broadcasted_iota(jnp.int32, (TOK, TOK), 0)
    s = lax.broadcasted_iota(jnp.int32, (TOK, TOK), 1)
    lower = jnp.where(s <= t, 1.0, 0.0).astype(BF16)
    parts = [dot(lower, x, 1, 1) for x in thirds(-rate_ref[...])]
    return parts[0] + (parts[1] + parts[2])


def decay_rows(rate_ref):
    s = lax.broadcasted_iota(jnp.int32, (TOK, TOK), 0)
    t = lax.broadcasted_iota(jnp.int32, (TOK, TOK), 1)
    upper = jnp.where(s <= t, 1.0, 0.0).astype(BF16)
    parts = [dot(x, upper, 1, 0) for x in thirds(-rate_ref[...])]
    return parts[0] + (parts[1] + parts[2])


def state_kernel(lengths_ref, rate_ref, key_ref, value_ref, out_ref):
    heads = rate_ref.shape[0]
    first = block_of() * TOK
    tail = begin_scalar(lengths_ref, first + TOK - 1)
    columns = decay_columns(rate_ref)
    rows = first + lax.broadcasted_iota(jnp.int32, (TOK, heads), 0)
    end = columns[TOK - 1 : TOK, :]
    weight = jnp.where(
        rows >= tail, jnp.exp(jnp.where(rows >= tail, end - columns, 0.0)), 0.0
    )
    carried = jnp.where(tail < first, jnp.exp(end), 0.0)
    half = HEAD_DIM // 2
    for h in range(heads):
        lanes = slice(h * HEAD_DIM, (h + 1) * HEAD_DIM)
        k = key_ref[:, lanes] * weight[:, h : h + 1]
        kh, kl = halves(k)
        vh, vl = halves(value_ref[:, lanes])
        inner = dot(
            jnp.concatenate([kh, kh, kl], axis=0),
            jnp.concatenate([vh, vl, vh], axis=0),
            0,
            0,
        )
        kept = jnp.broadcast_to(carried[:, h : h + 1], (8, HEAD_DIM))
        for i in range(2):
            out_ref[2 * h + i, :half] = inner[i * half : (i + 1) * half]
            out_ref[2 * h + i, half:] = kept


def prefix_kernel(lengths_ref, in_ref, out_ref):
    blocks, half = out_ref.shape[0], out_ref.shape[1]
    state = jnp.zeros(out_ref.shape[1:], F32)
    for i in range(blocks):
        out_ref[i] = state
        if i < blocks - 1:
            state = in_ref[i, half : half + 1, :] * state + in_ref[i, :half, :]


def intra_kernel(lengths_ref, rate_ref, query_ref, key_ref, value_ref, out_ref):
    heads = rate_ref.shape[0]
    first = block_of() * TOK
    columns = decay_columns(rate_ref)
    across = decay_rows(rate_ref)
    t = first + lax.broadcasted_iota(jnp.int32, (TOK, TOK), 0)
    s = first + lax.broadcasted_iota(jnp.int32, (TOK, TOK), 1)
    visible = (s <= t) & (s >= begins_of(lengths_ref, t))
    for h in range(heads):
        lanes = slice(h * HEAD_DIM, (h + 1) * HEAD_DIM)
        gap = jnp.where(visible, columns[:, h : h + 1] - across[h : h + 1, :], 0.0)
        weight = jnp.where(visible, jnp.exp(gap), 0.0)
        scores = dot6(query_ref[:, lanes], key_ref[:, lanes], 1, 1) * weight
        out_ref[:, lanes] = dot3(scores, value_ref[:, lanes], 1, 0)


def finish_kernel(
    lengths_ref, rate_ref, query_ref, state_ref, intra_ref, gate_ref, gain_ref, out_ref
):
    heads = rate_ref.shape[0]
    first = block_of() * TOK
    columns = decay_columns(rate_ref)
    rows = first + lax.broadcasted_iota(jnp.int32, (TOK, heads), 0)
    carried = begins_of(lengths_ref, rows) < first
    reach = jnp.where(carried, jnp.exp(columns), 0.0)
    for h in range(heads):
        lanes = slice(h * HEAD_DIM, (h + 1) * HEAD_DIM)
        x = intra_ref[:, lanes] + dot3(query_ref[:, lanes], state_ref[h], 1, 0) * reach[
            :, h : h + 1
        ]
        mean = jnp.mean(x * x, axis=1, keepdims=True)
        normed = x / jnp.sqrt(mean + NORM_EPS)
        gate = 1.0 / (1.0 + jnp.exp(-gate_ref[:, lanes]))
        out_ref[:, lanes] = normed * gain_ref[:, lanes] * gate


def shards(
    lin_query,
    lin_key,
    lin_value,
    lin_gate,
    decay_rate,
    norm_gain,
    sm_query,
    sm_key,
    sm_value,
    doc_lengths,
):
    rows, width = lin_query.shape
    heads = width // HEAD_DIM
    ys, zs = lax.axis_size("y"), lax.axis_size("z")
    blocks = ys * zs
    group = ("y", "head")
    out = jax.ShapeDtypeStruct
    forth, back = [], []
    for r in range(4):
        pairs = []
        for y in range(ys):
            for h in range(2):
                piece = (y + r) % 4
                pairs.append((2 * y + h, 2 * (2 * h + piece // 2) + piece % 2))
        forth.append(pairs)
        back.append([(b, a) for a, b in pairs])

    sliced = call(
        state_kernel, out((blocks, HEAD_DIM // 2 + 8, HEAD_DIM), F32), 4, limit=60
    )(doc_lengths, decay_rate, lin_key, lin_value)
    arrived = lax.all_to_all(sliced, ("y", "z"), 0, 0, tiled=True)

    inverse = np.zeros((1, HEAD_DIM), np.float32)
    inverse[0, :ROT_DIM] = np.tile(INVERSE, 2)
    sm_key, sliced = lax.optimization_barrier((sm_key, sliced))
    tables, *kv_pieces = call(
        kv_kernel,
        [out((3, rows, HEAD_DIM), F32)] + [out((rows, HEAD_DIM), F32)] * 4,
        4,
        limit=60,
    )(doc_lengths, jnp.asarray(inverse), sm_key, sm_value)
    kv_here = [lax.ppermute(p, group, forth[r]) for r, p in enumerate(kv_pieces)]

    up = [(i, (i + 1) % zs) for i in range(zs)]
    down = [(b, a) for a, b in up]
    own = jnp.stack(kv_here)
    up1 = lax.ppermute(own, "z", up)
    down1 = lax.ppermute(own, "z", down)

    sm_query, own = lax.optimization_barrier((sm_query, own))
    q_pieces = call(query_kernel, [out((rows, QUERIES), F32)] * 4, 3, limit=60)(
        doc_lengths, tables, sm_query
    )
    up1, down1, arrived, *second = lax.optimization_barrier(
        (up1, down1, arrived, *q_pieces[2:])
    )
    q_pieces = [*q_pieces[:2], *second]
    here = [lax.ppermute(p, group, forth[r]) for r, p in enumerate(q_pieces)]
    up2 = lax.ppermute(up1, "z", up)
    down2 = lax.ppermute(down1, "z", down)
    prefixes = call(prefix_kernel, out((blocks, HEAD_DIM // 2, HEAD_DIM), F32), 2)(
        doc_lengths, arrived
    )
    up2, down2, prefixes, lin_query, *here = lax.optimization_barrier(
        (up2, down2, prefixes, lin_query, *here)
    )
    intra = call(intra_kernel, out((rows, width), F32), 5)(
        doc_lengths, decay_rate, lin_query, lin_key, lin_value
    )
    up3 = lax.ppermute(up2, "z", up)
    down3 = lax.ppermute(down2, "z", down)
    up3, down3, prefixes, intra = lax.optimization_barrier((up3, down3, prefixes, intra))
    up4 = lax.ppermute(up3, "z", up)
    cross = [
        (2 * i + c, 2 * ((i - 1) % zs) + 1 - c) for i in range(zs) for c in range(2)
    ]
    theirs4 = lax.ppermute(down3, ("z", "head"), cross)
    near = [own, up1, down1, up2, down2, up3, down3]
    theirs = lax.ppermute(jnp.stack(near), "head", [(0, 1), (1, 0)])

    state = lax.all_to_all(prefixes, ("y", "z"), 0, 0, tiled=True)
    state = state.reshape(heads, HEAD_DIM, HEAD_DIM)

    keys = blocks * TOK
    mixed = call(
        softmax_kernel,
        [out((rows, 4 * HEAD_DIM), F32)] * 4,
        15,
        scratch=[
            pltpu.VMEM((keys, 384), BF16),
            pltpu.VMEM((keys, 256), BF16),
            pltpu.VMEM((4 * TOK, 384), BF16),
            pltpu.VMEM((keys // CHUNK, 4 * TOK, CHUNK), F32),
            pltpu.VMEM((4 * TOK, HEAD_DIM), F32),
            pltpu.VMEM((4 * TOK, HEAD_DIM), F32),
            pltpu.VMEM((4 * TOK, 2 * HEAD_DIM), F32),
        ],
        limit=60,
        flops=400_000_000_000,
        moved=8_000_000,
    )(
        doc_lengths, *here, *near, up4, theirs, theirs4
    )
    returned = [lax.ppermute(p, group, back[r]) for r, p in enumerate(mixed)]

    lin_out = call(finish_kernel, out((rows, width), F32), 7, limit=60)(
        doc_lengths,
        decay_rate,
        lin_query,
        state,
        intra,
        lin_gate,
        norm_gain.reshape(1, width),
    )
    lin_out, *returned = lax.optimization_barrier((lin_out, *returned))
    sm_out = call(place_kernel, out((rows, width), F32), 5)(doc_lengths, *returned)
    return (lin_out, sm_out)


def solution(mesh):
    sizes = mesh.shape
    ring = 4
    inner = Mesh(
        mesh.devices.reshape(ring, sizes["context"] // ring, sizes["head"], sizes["dp"]),
        ("y", "z", "head", "dp"),
    )
    tokens = ("dp", "y", "z")
    wide = P(tokens, "head")
    in_specs = (
        wide,
        wide,
        wide,
        wide,
        P("head", tokens),
        P("head"),
        wide,
        wide,
        wide,
        P("dp"),
    )
    return jax.shard_map(
        shards, mesh=inner, in_specs=in_specs, out_specs=(wide, wide), check_vma=False
    )
```

```python
import functools
import math

import jax
import jax.numpy as jnp
import numpy as np
from jax import lax
from jax.experimental import pallas as pl
from jax.experimental.pallas import tpu as pltpu
from jax.sharding import Mesh, PartitionSpec as P

HEAD_DIM = 128
ROT_DIM = 64
TOK = 128
DOCS = 16
CHUNK = 512
PIECES = (0, 1, -1, 2, -2, 3, -3, 4)
NEG = -1e30
GROUP = 8
QUERIES = GROUP * HEAD_DIM
ROPE_BASE = 10000000.0
NORM_EPS = 1e-05
F32 = jnp.float32
BF16 = jnp.bfloat16

INVERSE = np.power(
    ROPE_BASE, -(2.0 * np.arange(ROT_DIM // 2, dtype=np.float64)) / ROT_DIM
).astype(np.float32)

VMEM = pl.BlockSpec(memory_space=pltpu.VMEM)
SMEM = pl.BlockSpec(memory_space=pltpu.SMEM)


def built(kernel, out_shape, shapes, scratch=(), flops=1000, moved=1000, limit=20):
    def whole(shape):
        return pl.BlockSpec(shape, lambda i: (0,) * len(shape))

    many = isinstance(out_shape, (tuple, list))
    return pl.pallas_call(
        kernel,
        out_shape=out_shape,
        grid=(1,),
        in_specs=[SMEM] + [whole(shape) for shape in shapes],
        out_specs=[whole(o.shape) for o in out_shape] if many else whole(out_shape.shape),
        scratch_shapes=list(scratch),
        compiler_params=pltpu.CompilerParams(vmem_limit_bytes=limit << 20),
        cost_estimate=pl.CostEstimate(
            flops=flops, bytes_accessed=moved, transcendentals=0
        ),
    )


def call(kernel, out_shape, n_in, **options):
    def run(lengths, *arrays):
        return built(kernel, out_shape, [a.shape for a in arrays], **options)(lengths, *arrays)

    return run


def halves(x):
    high = x.astype(BF16)
    return high, (x - high.astype(F32)).astype(BF16)


def dot(a, b, ca, cb):
    return lax.dot_general(a, b, (((ca,), (cb,)), ((), ())), preferred_element_type=F32)


def dot3(a, b, ca, cb):
    ah, al = halves(a)
    bh, bl = halves(b)
    return dot(ah, bh, ca, cb) + (dot(ah, bl, ca, cb) + dot(al, bh, ca, cb))


def begins_of(lengths_ref, tokens):
    begin = jnp.zeros_like(tokens)
    start = jnp.int32(0)
    for d in range(DOCS - 1):
        start = start + lengths_ref[d]
        begin = jnp.where(tokens >= start, start, begin)
    return begin


def begin_scalar(lengths_ref, token):
    begin = jnp.int32(0)
    start = jnp.int32(0)
    for d in range(DOCS - 1):
        start = start + lengths_ref[d]
        begin = jnp.where(token >= start, start, begin)
    return begin


def block_of():
    return lax.axis_index("y") * lax.axis_size("z") + lax.axis_index("z")


def sent_in(r):
    return (lax.axis_index("y") // 2 + r) % 2


def row_of(r, core):
    return 2 * ((lax.axis_index("y") - r + 2) % 2) + core


def rope_tables(lengths_ref, inverse_ref, first):
    rows = first + lax.broadcasted_iota(jnp.int32, (TOK, HEAD_DIM), 0)
    lane = lax.broadcasted_iota(jnp.int32, (TOK, HEAD_DIM), 1)
    position = (rows - begins_of(lengths_ref, rows)).astype(F32)
    angle = position * inverse_ref[...]
    rotated = lane < ROT_DIM
    cosine = jnp.where(rotated, jnp.cos(angle), 1.0)
    sine = jnp.sin(angle)
    low = jnp.where(lane < ROT_DIM // 2, -sine, 0.0)
    high = jnp.where(rotated & (lane >= ROT_DIM // 2), sine, 0.0)
    return cosine, low, high


def rotated(x, tables):
    cosine, low, high = tables
    half = ROT_DIM // 2
    return (
        x * cosine
        + pltpu.roll(x, HEAD_DIM - half, 1) * low
        + pltpu.roll(x, half, 1) * high
    )


def kv_kernel(lengths_ref, inverse_ref, key_ref, value_ref, tables_ref, *pieces):
    tables = rope_tables(lengths_ref, inverse_ref, block_of() * TOK)
    for i in range(3):
        tables_ref[i] = tables[i]
    for r in range(2):
        at = pl.multiple_of(sent_in(r) * HEAD_DIM, HEAD_DIM)
        pieces[r][:, :HEAD_DIM] = rotated(key_ref[:, pl.ds(at, HEAD_DIM)], tables)
        pieces[r][:, HEAD_DIM:] = value_ref[:, pl.ds(at, HEAD_DIM)]


def query_kernel(lengths_ref, tables_ref, query_ref, *pieces):
    tables = [tables_ref[i] for i in range(3)]
    scale = math.log2(math.e) / math.sqrt(HEAD_DIM)
    for r in range(2):
        for n in range(GROUP):
            at = pl.multiple_of(sent_in(r) * QUERIES + n * HEAD_DIM, HEAD_DIM)
            x = query_ref[:, pl.ds(at, HEAD_DIM)]
            pieces[r][:, n * HEAD_DIM : (n + 1) * HEAD_DIM] = rotated(x, tables) * scale


def pack(mine, theirs, kcat, vcat):
    z, zs = lax.axis_index("z"), lax.axis_size("z")
    core = lax.axis_index("head")
    for i in range(8):
        source = (z - PIECES[i] + zs) % zs
        for own in (True, False):
            for r in range(2):
                if own:
                    x = mine[i][r]
                elif i < 7:
                    x = theirs[0][i, r]
                else:
                    x = theirs[1][r]
                row = row_of(r, core if own else 1 - core)
                at = pl.multiple_of((row * zs + source) * TOK, TOK)
                high, low = halves(x[:, :HEAD_DIM])
                kcat[pl.ds(at, TOK), 0:128] = high
                kcat[pl.ds(at, TOK), 128:256] = high
                kcat[pl.ds(at, TOK), 256:384] = low
                high, low = halves(x[:, HEAD_DIM:])
                vcat[pl.ds(at, TOK), 0:128] = high
                vcat[pl.ds(at, TOK), 128:256] = low


def softmax_kernel(lengths_ref, *refs):
    queries, mine, theirs, outs = refs[:2], refs[2:10], refs[10:12], refs[12:14]
    kcat, vcat = refs[14:16]
    pack(mine, theirs, kcat, vcat)
    for r in range(2):
        attend(r, lengths_ref, queries[r], kcat, vcat, outs[r], *refs[16:])


def attend(r, lengths_ref, query_ref, kcat, vcat, out_ref, *scratch):
    qcat, s_ref, m_ref, l_ref, acc_ref = scratch
    block = row_of(r, lax.axis_index("head")) * lax.axis_size("z") + lax.axis_index("z")
    first = block * TOK
    for n in range(GROUP):
        qh, ql = halves(query_ref[:, n * HEAD_DIM : (n + 1) * HEAD_DIM])
        qcat[n * TOK : (n + 1) * TOK, 0:128] = qh
        qcat[n * TOK : (n + 1) * TOK, 128:256] = ql
        qcat[n * TOK : (n + 1) * TOK, 256:384] = qh
    low = begin_scalar(lengths_ref, first) // CHUNK
    high = first // CHUNK + 1
    inner = (begin_scalar(lengths_ref, first + TOK - 1) + CHUNK - 1) // CHUNK
    inner = jnp.minimum(inner, high)
    outer = jnp.maximum(inner, high - 1)
    m_ref[...] = jnp.full_like(m_ref, NEG)
    l_ref[...] = jnp.zeros_like(l_ref)
    acc_ref[...] = jnp.zeros_like(acc_ref)

    def score(j, masked):
        at = pl.multiple_of(j * CHUNK, CHUNK)
        s = dot(qcat[...], kcat[pl.ds(at, CHUNK), :], 1, 1)
        if masked:
            rows = first + lax.broadcasted_iota(jnp.int32, (TOK, CHUNK), 0)
            keys = at + lax.broadcasted_iota(jnp.int32, (TOK, CHUNK), 1)
            begin = begins_of(
                lengths_ref, first + lax.broadcasted_iota(jnp.int32, (TOK, 1), 0)
            )
            visible = (keys >= begin) & (keys <= rows)
            s = jnp.where(visible[None], s.reshape(GROUP, TOK, CHUNK), NEG)
            s = s.reshape(GROUP * TOK, CHUNK)
        s_ref[j] = s
        top = s[:, :HEAD_DIM]
        for i in range(1, CHUNK // HEAD_DIM):
            top = jnp.maximum(top, s[:, i * HEAD_DIM : (i + 1) * HEAD_DIM])
        m_ref[...] = jnp.maximum(m_ref[...], top)

    pl.loop(low, inner)(lambda j: score(j, True))
    pl.loop(inner, outer)(lambda j: score(j, False))
    pl.loop(outer, high)(lambda j: score(j, True))

    top = jnp.max(m_ref[...], axis=1, keepdims=True)
    m_ref[...] = jnp.broadcast_to(top, m_ref.shape)

    def mix(j):
        at = pl.multiple_of(j * CHUNK, CHUNK)
        top = m_ref[...]
        highs, lows, total = [], [], l_ref[...]
        for i in range(CHUNK // HEAD_DIM):
            p = jnp.exp2(s_ref[j, :, i * HEAD_DIM : (i + 1) * HEAD_DIM] - top)
            total = total + p
            ph, pl_ = halves(p)
            highs.append(ph)
            lows.append(pl_)
        l_ref[...] = total
        v = vcat[pl.ds(at, CHUNK), :]
        p = jnp.concatenate(highs + lows, axis=1)
        acc_ref[...] += dot(p, jnp.concatenate([v, v], axis=0), 1, 0)

    pl.loop(low, high)(mix)

    total = jnp.sum(l_ref[...], axis=1, keepdims=True)
    mixed = (acc_ref[:, :HEAD_DIM] + acc_ref[:, HEAD_DIM:]) / total
    for n in range(GROUP):
        out_ref[:, n * HEAD_DIM : (n + 1) * HEAD_DIM] = mixed[n * TOK : (n + 1) * TOK]


def place_kernel(lengths_ref, *refs):
    pieces, out_ref = refs[:2], refs[2]
    for r in range(2):
        at = pl.multiple_of(sent_in(r) * QUERIES, QUERIES)
        out_ref[:, pl.ds(at, QUERIES)] = pieces[r][...]


def thirds(x):
    high = x.astype(BF16)
    rest = x - high.astype(F32)
    mid = rest.astype(BF16)
    return high, mid, (rest - mid.astype(F32)).astype(BF16)


def dot6(a, b, ca, cb):
    ah, am, al = thirds(a)
    bh, bm, bl = thirds(b)
    return dot(
        jnp.concatenate([ah, am, ah, al, am, ah], axis=ca),
        jnp.concatenate([bl, bm, bm, bh, bh, bh], axis=cb),
        ca,
        cb,
    )


def decay_columns(rate_ref):
    t = lax.broadcasted_iota(jnp.int32, (TOK, TOK), 0)
    s = lax.broadcasted_iota(jnp.int32, (TOK, TOK), 1)
    lower = jnp.where(s <= t, 1.0, 0.0).astype(BF16)
    parts = [dot(lower, x, 1, 1) for x in thirds(-rate_ref[...])]
    return parts[0] + (parts[1] + parts[2])


def decay_rows(rate_ref):
    s = lax.broadcasted_iota(jnp.int32, (TOK, TOK), 0)
    t = lax.broadcasted_iota(jnp.int32, (TOK, TOK), 1)
    upper = jnp.where(s <= t, 1.0, 0.0).astype(BF16)
    parts = [dot(x, upper, 1, 0) for x in thirds(-rate_ref[...])]
    return parts[0] + (parts[1] + parts[2])


def state_kernel(lengths_ref, rate_ref, key_ref, value_ref, out_ref):
    heads = rate_ref.shape[0]
    first = block_of() * TOK
    tail = begin_scalar(lengths_ref, first + TOK - 1)
    columns = decay_columns(rate_ref)
    rows = first + lax.broadcasted_iota(jnp.int32, (TOK, heads), 0)
    end = columns[TOK - 1 : TOK, :]
    weight = jnp.where(
        rows >= tail, jnp.exp(jnp.where(rows >= tail, end - columns, 0.0)), 0.0
    )
    carried = jnp.where(tail < first, jnp.exp(end), 0.0)
    half = HEAD_DIM // 2
    for h in range(heads):
        lanes = slice(h * HEAD_DIM, (h + 1) * HEAD_DIM)
        k = key_ref[:, lanes] * weight[:, h : h + 1]
        kh, kl = halves(k)
        vh, vl = halves(value_ref[:, lanes])
        inner = dot(
            jnp.concatenate([kh, kh, kl], axis=0),
            jnp.concatenate([vh, vl, vh], axis=0),
            0,
            0,
        )
        kept = jnp.broadcast_to(carried[:, h : h + 1], (8, HEAD_DIM))
        for i in range(2):
            out_ref[2 * h + i, :half] = inner[i * half : (i + 1) * half]
            out_ref[2 * h + i, half:] = kept


def prefix_kernel(lengths_ref, in_ref, out_ref):
    blocks, half = out_ref.shape[0], out_ref.shape[1]
    state = jnp.zeros(out_ref.shape[1:], F32)
    for i in range(blocks):
        out_ref[i] = state
        if i < blocks - 1:
            state = in_ref[i, half : half + 1, :] * state + in_ref[i, :half, :]


def intra_kernel(lengths_ref, rate_ref, query_ref, key_ref, value_ref, out_ref):
    heads = rate_ref.shape[0]
    first = block_of() * TOK
    columns = decay_columns(rate_ref)
    across = decay_rows(rate_ref)
    t = first + lax.broadcasted_iota(jnp.int32, (TOK, TOK), 0)
    s = first + lax.broadcasted_iota(jnp.int32, (TOK, TOK), 1)
    visible = (s <= t) & (s >= begins_of(lengths_ref, t))
    for h in range(heads):
        lanes = slice(h * HEAD_DIM, (h + 1) * HEAD_DIM)
        gap = jnp.where(visible, columns[:, h : h + 1] - across[h : h + 1, :], 0.0)
        weight = jnp.where(visible, jnp.exp(gap), 0.0)
        scores = dot6(query_ref[:, lanes], key_ref[:, lanes], 1, 1) * weight
        sh, sl = halves(scores)
        vh, vl = halves(value_ref[:, lanes])
        out_ref[:, lanes] = dot(
            jnp.concatenate([sh, sl, sh], axis=1), jnp.concatenate([vh, vh, vl], axis=0), 1, 0
        )


def finish_kernel(
    lengths_ref, rate_ref, query_ref, state_ref, intra_ref, gate_ref, gain_ref, out_ref
):
    heads = rate_ref.shape[0]
    first = block_of() * TOK
    columns = decay_columns(rate_ref)
    rows = first + lax.broadcasted_iota(jnp.int32, (TOK, heads), 0)
    carried = begins_of(lengths_ref, rows) < first
    reach = jnp.where(carried, jnp.exp(columns), 0.0)
    for h in range(heads):
        lanes = slice(h * HEAD_DIM, (h + 1) * HEAD_DIM)
        x = intra_ref[:, lanes] + dot3(query_ref[:, lanes], state_ref[h], 1, 0) * reach[
            :, h : h + 1
        ]
        mean = jnp.mean(x * x, axis=1, keepdims=True)
        normed = x / jnp.sqrt(mean + NORM_EPS)
        gate = 1.0 / (1.0 + jnp.exp(-gate_ref[:, lanes]))
        out_ref[:, lanes] = normed * gain_ref[:, lanes] * gate


def shards(
    lin_query,
    lin_key,
    lin_value,
    lin_gate,
    decay_rate,
    norm_gain,
    sm_query,
    sm_key,
    sm_value,
    doc_lengths,
):
    rows, width = lin_query.shape
    heads = width // HEAD_DIM
    ys, zs = lax.axis_size("y"), lax.axis_size("z")
    blocks = ys * zs
    group = ("y", "head")
    out = jax.ShapeDtypeStruct
    forth, back = [], []
    for r in range(2):
        pairs = [
            (2 * y + h, 2 * (2 * h + (y // 2 + r) % 2) + y % 2)
            for y in range(ys)
            for h in range(2)
        ]
        forth.append(pairs)
        back.append([(b, a) for a, b in pairs])

    sliced = call(
        state_kernel, out((blocks, HEAD_DIM // 2 + 8, HEAD_DIM), F32), 4, limit=60
    )(doc_lengths, decay_rate, lin_key, lin_value)
    arrived = lax.all_to_all(sliced, ("y", "z"), 0, 0, tiled=True)

    inverse = np.zeros((1, HEAD_DIM), np.float32)
    inverse[0, :ROT_DIM] = np.tile(INVERSE, 2)
    sm_key, sliced = lax.optimization_barrier((sm_key, sliced))
    tables, *kv_pieces = call(
        kv_kernel,
        [out((3, rows, HEAD_DIM), F32)] + [out((rows, 2 * HEAD_DIM), F32)] * 2,
        4,
        limit=60,
    )(doc_lengths, jnp.asarray(inverse), sm_key, sm_value)
    kv_here = [lax.ppermute(p, group, forth[r]) for r, p in enumerate(kv_pieces)]

    up = [(i, (i + 1) % zs) for i in range(zs)]
    down = [(b, a) for a, b in up]
    own = jnp.stack(kv_here)
    up1 = lax.ppermute(own, "z", up)
    down1 = lax.ppermute(own, "z", down)

    sm_query, lin_query, own = lax.optimization_barrier((sm_query, lin_query, own))
    q_pieces = call(query_kernel, [out((rows, QUERIES), F32)] * 2, 3, limit=60)(
        doc_lengths, tables, sm_query
    )
    here = [lax.ppermute(p, group, forth[r]) for r, p in enumerate(q_pieces)]
    intra = call(intra_kernel, out((rows, width), F32), 5)(
        doc_lengths, decay_rate, lin_query, lin_key, lin_value
    )
    up1, down1, arrived, intra = lax.optimization_barrier((up1, down1, arrived, intra))
    up2 = lax.ppermute(up1, "z", up)
    down2 = lax.ppermute(down1, "z", down)
    prefixes = call(prefix_kernel, out((blocks, HEAD_DIM // 2, HEAD_DIM), F32), 2)(
        doc_lengths, arrived
    )
    up2, down2, prefixes, *here = lax.optimization_barrier((up2, down2, prefixes, *here))
    up3 = lax.ppermute(up2, "z", up)
    down3 = lax.ppermute(down2, "z", down)
    up3, down3, prefixes = lax.optimization_barrier((up3, down3, prefixes))
    up4 = lax.ppermute(up3, "z", up)
    cross = [
        (2 * i + c, 2 * ((i - 1) % zs) + 1 - c) for i in range(zs) for c in range(2)
    ]
    theirs4 = lax.ppermute(down3, ("z", "head"), cross)
    near = [own, up1, down1, up2, down2, up3, down3]
    theirs = lax.ppermute(jnp.stack(near), "head", [(0, 1), (1, 0)])

    state = lax.all_to_all(prefixes, ("y", "z"), 0, 0, tiled=True)
    state = state.reshape(heads, HEAD_DIM, HEAD_DIM)

    keys = blocks * TOK
    mixed = call(
        softmax_kernel,
        [out((rows, QUERIES), F32)] * 2,
        13,
        scratch=[
            pltpu.VMEM((keys, 384), BF16),
            pltpu.VMEM((keys, 256), BF16),
            pltpu.VMEM((GROUP * TOK, 384), BF16),
            pltpu.VMEM((keys // CHUNK, GROUP * TOK, CHUNK), F32),
            pltpu.VMEM((GROUP * TOK, HEAD_DIM), F32),
            pltpu.VMEM((GROUP * TOK, HEAD_DIM), F32),
            pltpu.VMEM((GROUP * TOK, 2 * HEAD_DIM), F32),
        ],
        limit=60,
        flops=400_000_000_000,
        moved=8_000_000,
    )(
        doc_lengths, *here, *near, up4, theirs, theirs4
    )
    returned = [lax.ppermute(p, group, back[r]) for r, p in enumerate(mixed)]

    lin_out = call(finish_kernel, out((rows, width), F32), 7)(
        doc_lengths,
        decay_rate,
        lin_query,
        state,
        intra,
        lin_gate,
        norm_gain.reshape(1, width),
    )
    lin_out, *returned = lax.optimization_barrier((lin_out, *returned))
    sm_out = call(place_kernel, out((rows, width), F32), 3)(doc_lengths, *returned)
    return (lin_out, sm_out)


def solution(mesh):
    sizes = mesh.shape
    ring = 4
    inner = Mesh(
        mesh.devices.reshape(ring, sizes["context"] // ring, sizes["head"], sizes["dp"]),
        ("y", "z", "head", "dp"),
    )
    tokens = ("dp", "y", "z")
    wide = P(tokens, "head")
    in_specs = (
        wide,
        wide,
        wide,
        wide,
        P("head", tokens),
        P("head"),
        wide,
        wide,
        wide,
        P("dp"),
    )
    return jax.shard_map(
        shards, mesh=inner, in_specs=in_specs, out_specs=(wide, wide), check_vma=False
    )
```

```python
import functools
import math

import jax
import jax.numpy as jnp
import numpy as np
from jax import lax
from jax.experimental import pallas as pl
from jax.experimental.pallas import tpu as pltpu
from jax.sharding import Mesh, PartitionSpec as P

HEAD_DIM = 128
ROT_DIM = 64
TOK = 128
DOCS = 16
CHUNK = 512
PIECES = (0, 1, -1, 2, -2, 3, -3, 4)
NEG = -1e30
GROUP = 8
QUERIES = GROUP * HEAD_DIM
ROPE_BASE = 10000000.0
NORM_EPS = 1e-05
F32 = jnp.float32
BF16 = jnp.bfloat16

INVERSE = np.power(
    ROPE_BASE, -(2.0 * np.arange(ROT_DIM // 2, dtype=np.float64)) / ROT_DIM
).astype(np.float32)

VMEM = pl.BlockSpec(memory_space=pltpu.VMEM)
SMEM = pl.BlockSpec(memory_space=pltpu.SMEM)


def built(kernel, out_shape, shapes, scratch=(), flops=1000, moved=1000, limit=20):
    def whole(shape):
        return pl.BlockSpec(shape, lambda i: (0,) * len(shape))

    many = isinstance(out_shape, (tuple, list))
    return pl.pallas_call(
        kernel,
        out_shape=out_shape,
        grid=(1,),
        in_specs=[SMEM] + [whole(shape) for shape in shapes],
        out_specs=[whole(o.shape) for o in out_shape] if many else whole(out_shape.shape),
        scratch_shapes=list(scratch),
        compiler_params=pltpu.CompilerParams(vmem_limit_bytes=limit << 20),
        cost_estimate=pl.CostEstimate(
            flops=flops, bytes_accessed=moved, transcendentals=0
        ),
    )


def halved(kernel, out, out_axis, arrays, axes):
    def half(shape, axis):
        block = tuple(n // 2 if d == axis else n for d, n in enumerate(shape))
        return pl.BlockSpec(
            block, lambda i: tuple(i if d == axis else 0 for d in range(len(shape)))
        )

    return pl.pallas_call(
        kernel,
        out_shape=out,
        grid=(2,),
        in_specs=[SMEM] + [half(a.shape, axis) for a, axis in zip(arrays[1:], axes)],
        out_specs=half(out.shape, out_axis),
        compiler_params=pltpu.CompilerParams(vmem_limit_bytes=60 << 20),
        cost_estimate=pl.CostEstimate(flops=1000, bytes_accessed=1000, transcendentals=0),
    )(*arrays)


def call(kernel, out_shape, n_in, **options):
    def run(lengths, *arrays):
        return built(kernel, out_shape, [a.shape for a in arrays], **options)(lengths, *arrays)

    return run


def halves(x):
    high = x.astype(BF16)
    return high, (x - high.astype(F32)).astype(BF16)


def dot(a, b, ca, cb):
    return lax.dot_general(a, b, (((ca,), (cb,)), ((), ())), preferred_element_type=F32)


def dot3(a, b, ca, cb):
    ah, al = halves(a)
    bh, bl = halves(b)
    return dot(ah, bh, ca, cb) + (dot(ah, bl, ca, cb) + dot(al, bh, ca, cb))


def begins_of(lengths_ref, tokens):
    begin = jnp.zeros_like(tokens)
    start = jnp.int32(0)
    for d in range(DOCS - 1):
        start = start + lengths_ref[d]
        begin = jnp.where(tokens >= start, start, begin)
    return begin


def begin_scalar(lengths_ref, token):
    begin = jnp.int32(0)
    start = jnp.int32(0)
    for d in range(DOCS - 1):
        start = start + lengths_ref[d]
        begin = jnp.where(token >= start, start, begin)
    return begin


def block_of():
    return lax.axis_index("y") * lax.axis_size("z") + lax.axis_index("z")


def sent_in(r):
    return (lax.axis_index("y") // 2 + r) % 2


def row_of(r, core):
    return 2 * ((lax.axis_index("y") - r + 2) % 2) + core


def rope_tables(lengths_ref, inverse_ref, first):
    rows = first + lax.broadcasted_iota(jnp.int32, (TOK, HEAD_DIM), 0)
    lane = lax.broadcasted_iota(jnp.int32, (TOK, HEAD_DIM), 1)
    position = (rows - begins_of(lengths_ref, rows)).astype(F32)
    angle = position * inverse_ref[...]
    rotated = lane < ROT_DIM
    cosine = jnp.where(rotated, jnp.cos(angle), 1.0)
    sine = jnp.sin(angle)
    low = jnp.where(lane < ROT_DIM // 2, -sine, 0.0)
    high = jnp.where(rotated & (lane >= ROT_DIM // 2), sine, 0.0)
    return cosine, low, high


def rotated(x, tables):
    cosine, low, high = tables
    half = ROT_DIM // 2
    return (
        x * cosine
        + pltpu.roll(x, HEAD_DIM - half, 1) * low
        + pltpu.roll(x, half, 1) * high
    )


def kv_kernel(lengths_ref, inverse_ref, key_ref, value_ref, tables_ref, *pieces):
    tables = rope_tables(lengths_ref, inverse_ref, block_of() * TOK)
    for i in range(3):
        tables_ref[i] = tables[i]
    for r in range(2):
        at = pl.multiple_of(sent_in(r) * HEAD_DIM, HEAD_DIM)
        pieces[r][:, :HEAD_DIM] = rotated(key_ref[:, pl.ds(at, HEAD_DIM)], tables)
        pieces[r][:, HEAD_DIM:] = value_ref[:, pl.ds(at, HEAD_DIM)]


def query_kernel(lengths_ref, tables_ref, query_ref, *pieces):
    tables = [tables_ref[i] for i in range(3)]
    scale = math.log2(math.e) / math.sqrt(HEAD_DIM)
    for r in range(2):
        for n in range(GROUP):
            at = pl.multiple_of(sent_in(r) * QUERIES + n * HEAD_DIM, HEAD_DIM)
            x = query_ref[:, pl.ds(at, HEAD_DIM)]
            pieces[r][:, n * HEAD_DIM : (n + 1) * HEAD_DIM] = rotated(x, tables) * scale


def pack(mine, theirs, kcat, vcat):
    z, zs = lax.axis_index("z"), lax.axis_size("z")
    core = lax.axis_index("head")
    for i in range(8):
        source = (z - PIECES[i] + zs) % zs
        for own in (True, False):
            for r in range(2):
                if own:
                    x = mine[i][r]
                elif i < 7:
                    x = theirs[0][i, r]
                else:
                    x = theirs[1][r]
                row = row_of(r, core if own else 1 - core)
                at = pl.multiple_of((row * zs + source) * TOK, TOK)
                high, low = halves(x[:, :HEAD_DIM])
                kcat[pl.ds(at, TOK), 0:128] = high
                kcat[pl.ds(at, TOK), 128:256] = high
                kcat[pl.ds(at, TOK), 256:384] = low
                high, low = halves(x[:, HEAD_DIM:])
                vcat[pl.ds(at, TOK), 0:128] = high
                vcat[pl.ds(at, TOK), 128:256] = low


def softmax_kernel(lengths_ref, *refs):
    queries, mine, theirs, outs = refs[:2], refs[2:10], refs[10:12], refs[12:14]
    kcat, vcat = refs[14:16]
    pack(mine, theirs, kcat, vcat)
    for r in range(2):
        attend(r, lengths_ref, queries[r], kcat, vcat, outs[r], *refs[16:])


def attend(r, lengths_ref, query_ref, kcat, vcat, out_ref, *scratch):
    qcat, s_ref, m_ref, l_ref, acc_ref = scratch
    block = row_of(r, lax.axis_index("head")) * lax.axis_size("z") + lax.axis_index("z")
    first = block * TOK
    for n in range(GROUP):
        qh, ql = halves(query_ref[:, n * HEAD_DIM : (n + 1) * HEAD_DIM])
        qcat[n * TOK : (n + 1) * TOK, 0:128] = qh
        qcat[n * TOK : (n + 1) * TOK, 128:256] = ql
        qcat[n * TOK : (n + 1) * TOK, 256:384] = qh
    low = begin_scalar(lengths_ref, first) // CHUNK
    high = first // CHUNK + 1
    inner = (begin_scalar(lengths_ref, first + TOK - 1) + CHUNK - 1) // CHUNK
    inner = jnp.minimum(inner, high)
    outer = jnp.maximum(inner, high - 1)
    m_ref[...] = jnp.full_like(m_ref, NEG)
    l_ref[...] = jnp.zeros_like(l_ref)
    acc_ref[...] = jnp.zeros_like(acc_ref)

    def score(j, masked):
        at = pl.multiple_of(j * CHUNK, CHUNK)
        s = dot(qcat[...], kcat[pl.ds(at, CHUNK), :], 1, 1)
        if masked:
            rows = first + lax.broadcasted_iota(jnp.int32, (TOK, CHUNK), 0)
            keys = at + lax.broadcasted_iota(jnp.int32, (TOK, CHUNK), 1)
            begin = begins_of(
                lengths_ref, first + lax.broadcasted_iota(jnp.int32, (TOK, 1), 0)
            )
            visible = (keys >= begin) & (keys <= rows)
            s = jnp.where(visible[None], s.reshape(GROUP, TOK, CHUNK), NEG)
            s = s.reshape(GROUP * TOK, CHUNK)
        s_ref[j] = s
        top = s[:, :HEAD_DIM]
        for i in range(1, CHUNK // HEAD_DIM):
            top = jnp.maximum(top, s[:, i * HEAD_DIM : (i + 1) * HEAD_DIM])
        m_ref[...] = jnp.maximum(m_ref[...], top)

    pl.loop(low, inner)(lambda j: score(j, True))
    pl.loop(inner, outer)(lambda j: score(j, False))
    pl.loop(outer, high)(lambda j: score(j, True))

    top = jnp.max(m_ref[...], axis=1, keepdims=True)
    m_ref[...] = jnp.broadcast_to(top, m_ref.shape)

    def mix(j):
        at = pl.multiple_of(j * CHUNK, CHUNK)
        top = m_ref[...]
        highs, lows, total = [], [], l_ref[...]
        for i in range(CHUNK // HEAD_DIM):
            p = jnp.exp2(s_ref[j, :, i * HEAD_DIM : (i + 1) * HEAD_DIM] - top)
            total = total + p
            ph, pl_ = halves(p)
            highs.append(ph)
            lows.append(pl_)
        l_ref[...] = total
        v = vcat[pl.ds(at, CHUNK), :]
        p = jnp.concatenate(highs + lows, axis=1)
        acc_ref[...] += dot(p, jnp.concatenate([v, v], axis=0), 1, 0)

    pl.loop(low, high)(mix)

    total = jnp.sum(l_ref[...], axis=1, keepdims=True)
    mixed = (acc_ref[:, :HEAD_DIM] + acc_ref[:, HEAD_DIM:]) / total
    for n in range(GROUP):
        out_ref[:, n * HEAD_DIM : (n + 1) * HEAD_DIM] = mixed[n * TOK : (n + 1) * TOK]


def place_kernel(lengths_ref, *refs):
    pieces, out_ref = refs[:2], refs[2]
    for r in range(2):
        at = pl.multiple_of(sent_in(r) * QUERIES, QUERIES)
        out_ref[:, pl.ds(at, QUERIES)] = pieces[r][...]


def thirds(x):
    high = x.astype(BF16)
    rest = x - high.astype(F32)
    mid = rest.astype(BF16)
    return high, mid, (rest - mid.astype(F32)).astype(BF16)


def dot6(a, b, ca, cb):
    ah, am, al = thirds(a)
    bh, bm, bl = thirds(b)
    return dot(
        jnp.concatenate([ah, am, ah, al, am, ah], axis=ca),
        jnp.concatenate([bl, bm, bm, bh, bh, bh], axis=cb),
        ca,
        cb,
    )


def decay_columns(rate_ref):
    t = lax.broadcasted_iota(jnp.int32, (TOK, TOK), 0)
    s = lax.broadcasted_iota(jnp.int32, (TOK, TOK), 1)
    lower = jnp.where(s <= t, 1.0, 0.0).astype(BF16)
    parts = [dot(lower, x, 1, 1) for x in thirds(-rate_ref[...])]
    return parts[0] + (parts[1] + parts[2])


def decay_rows(rate_ref):
    s = lax.broadcasted_iota(jnp.int32, (TOK, TOK), 0)
    t = lax.broadcasted_iota(jnp.int32, (TOK, TOK), 1)
    upper = jnp.where(s <= t, 1.0, 0.0).astype(BF16)
    parts = [dot(x, upper, 1, 0) for x in thirds(-rate_ref[...])]
    return parts[0] + (parts[1] + parts[2])


def state_kernel(lengths_ref, rate_ref, key_ref, value_ref, out_ref):
    heads = rate_ref.shape[0]
    first = block_of() * TOK
    tail = begin_scalar(lengths_ref, first + TOK - 1)
    columns = decay_columns(rate_ref)
    rows = first + lax.broadcasted_iota(jnp.int32, (TOK, heads), 0)
    end = columns[TOK - 1 : TOK, :]
    weight = jnp.where(
        rows >= tail, jnp.exp(jnp.where(rows >= tail, end - columns, 0.0)), 0.0
    )
    carried = jnp.where(tail < first, jnp.exp(end), 0.0)
    half = HEAD_DIM // 2
    for h in range(heads):
        lanes = slice(h * HEAD_DIM, (h + 1) * HEAD_DIM)
        k = key_ref[:, lanes] * weight[:, h : h + 1]
        kh, kl = halves(k)
        vh, vl = halves(value_ref[:, lanes])
        inner = dot(
            jnp.concatenate([kh, kh, kl], axis=0),
            jnp.concatenate([vh, vl, vh], axis=0),
            0,
            0,
        )
        kept = jnp.broadcast_to(carried[:, h : h + 1], (8, HEAD_DIM))
        for i in range(2):
            out_ref[2 * h + i, :half] = inner[i * half : (i + 1) * half]
            out_ref[2 * h + i, half:] = kept


def prefix_kernel(lengths_ref, in_ref, out_ref):
    blocks, half = out_ref.shape[0], out_ref.shape[1]
    state = jnp.zeros(out_ref.shape[1:], F32)
    for i in range(blocks):
        out_ref[i] = state
        if i < blocks - 1:
            state = in_ref[i, half : half + 1, :] * state + in_ref[i, :half, :]


def intra_kernel(lengths_ref, rate_ref, query_ref, key_ref, value_ref, out_ref):
    heads = rate_ref.shape[0]
    first = block_of() * TOK
    columns = decay_columns(rate_ref)
    across = decay_rows(rate_ref)
    t = first + lax.broadcasted_iota(jnp.int32, (TOK, TOK), 0)
    s = first + lax.broadcasted_iota(jnp.int32, (TOK, TOK), 1)
    visible = (s <= t) & (s >= begins_of(lengths_ref, t))
    for h in range(heads):
        lanes = slice(h * HEAD_DIM, (h + 1) * HEAD_DIM)
        gap = jnp.where(visible, columns[:, h : h + 1] - across[h : h + 1, :], 0.0)
        weight = jnp.where(visible, jnp.exp(gap), 0.0)
        scores = dot6(query_ref[:, lanes], key_ref[:, lanes], 1, 1) * weight
        sh, sl = halves(scores)
        vh, vl = halves(value_ref[:, lanes])
        out_ref[:, lanes] = dot(
            jnp.concatenate([sh, sl, sh], axis=1), jnp.concatenate([vh, vh, vl], axis=0), 1, 0
        )


def finish_kernel(
    lengths_ref, rate_ref, query_ref, state_ref, intra_ref, gate_ref, gain_ref, out_ref
):
    heads = rate_ref.shape[0]
    first = block_of() * TOK
    columns = decay_columns(rate_ref)
    rows = first + lax.broadcasted_iota(jnp.int32, (TOK, heads), 0)
    carried = begins_of(lengths_ref, rows) < first
    reach = jnp.where(carried, jnp.exp(columns), 0.0)
    for h in range(heads):
        lanes = slice(h * HEAD_DIM, (h + 1) * HEAD_DIM)
        x = intra_ref[:, lanes] + dot3(query_ref[:, lanes], state_ref[h], 1, 0) * reach[
            :, h : h + 1
        ]
        mean = jnp.mean(x * x, axis=1, keepdims=True)
        normed = x / jnp.sqrt(mean + NORM_EPS)
        gate = 1.0 / (1.0 + jnp.exp(-gate_ref[:, lanes]))
        out_ref[:, lanes] = normed * gain_ref[:, lanes] * gate


def shards(
    lin_query,
    lin_key,
    lin_value,
    lin_gate,
    decay_rate,
    norm_gain,
    sm_query,
    sm_key,
    sm_value,
    doc_lengths,
):
    rows, width = lin_query.shape
    heads = width // HEAD_DIM
    ys, zs = lax.axis_size("y"), lax.axis_size("z")
    blocks = ys * zs
    group = ("y", "head")
    out = jax.ShapeDtypeStruct
    forth, back = [], []
    for r in range(2):
        pairs = [
            (2 * y + h, 2 * (2 * h + (y // 2 + r) % 2) + y % 2)
            for y in range(ys)
            for h in range(2)
        ]
        forth.append(pairs)
        back.append([(b, a) for a, b in pairs])

    sliced = halved(
        state_kernel,
        out((blocks, HEAD_DIM // 2 + 8, HEAD_DIM), F32),
        0,
        (doc_lengths, decay_rate, lin_key, lin_value),
        (0, 1, 1),
    )
    arrived = lax.all_to_all(sliced, ("y", "z"), 0, 0, tiled=True)

    inverse = np.zeros((1, HEAD_DIM), np.float32)
    inverse[0, :ROT_DIM] = np.tile(INVERSE, 2)
    sm_key, sliced = lax.optimization_barrier((sm_key, sliced))
    tables, *kv_pieces = call(
        kv_kernel,
        [out((3, rows, HEAD_DIM), F32)] + [out((rows, 2 * HEAD_DIM), F32)] * 2,
        4,
        limit=60,
    )(doc_lengths, jnp.asarray(inverse), sm_key, sm_value)
    kv_here = [lax.ppermute(p, group, forth[r]) for r, p in enumerate(kv_pieces)]

    up = [(i, (i + 1) % zs) for i in range(zs)]
    down = [(b, a) for a, b in up]
    own = jnp.stack(kv_here)
    up1 = lax.ppermute(own, "z", up)
    down1 = lax.ppermute(own, "z", down)

    sm_query, lin_query, own = lax.optimization_barrier((sm_query, lin_query, own))
    q_pieces = call(query_kernel, [out((rows, QUERIES), F32)] * 2, 3, limit=60)(
        doc_lengths, tables, sm_query
    )
    here = [lax.ppermute(p, group, forth[r]) for r, p in enumerate(q_pieces)]
    intra = call(intra_kernel, out((rows, width), F32), 5)(
        doc_lengths, decay_rate, lin_query, lin_key, lin_value
    )
    up1, down1, arrived, intra = lax.optimization_barrier((up1, down1, arrived, intra))
    up2 = lax.ppermute(up1, "z", up)
    down2 = lax.ppermute(down1, "z", down)
    prefixes = call(prefix_kernel, out((blocks, HEAD_DIM // 2, HEAD_DIM), F32), 2)(
        doc_lengths, arrived
    )
    up2, down2, prefixes, *here = lax.optimization_barrier((up2, down2, prefixes, *here))
    up3 = lax.ppermute(up2, "z", up)
    down3 = lax.ppermute(down2, "z", down)
    up3, down3, prefixes = lax.optimization_barrier((up3, down3, prefixes))
    up4 = lax.ppermute(up3, "z", up)
    cross = [
        (2 * i + c, 2 * ((i - 1) % zs) + 1 - c) for i in range(zs) for c in range(2)
    ]
    theirs4 = lax.ppermute(down3, ("z", "head"), cross)
    near = [own, up1, down1, up2, down2, up3, down3]
    theirs = lax.ppermute(jnp.stack(near), "head", [(0, 1), (1, 0)])

    state = lax.all_to_all(prefixes, ("y", "z"), 0, 0, tiled=True)
    state = state.reshape(heads, HEAD_DIM, HEAD_DIM)

    keys = blocks * TOK
    mixed = call(
        softmax_kernel,
        [out((rows, QUERIES), F32)] * 2,
        13,
        scratch=[
            pltpu.VMEM((keys, 384), BF16),
            pltpu.VMEM((keys, 256), BF16),
            pltpu.VMEM((GROUP * TOK, 384), BF16),
            pltpu.VMEM((keys // CHUNK, GROUP * TOK, CHUNK), F32),
            pltpu.VMEM((GROUP * TOK, HEAD_DIM), F32),
            pltpu.VMEM((GROUP * TOK, HEAD_DIM), F32),
            pltpu.VMEM((GROUP * TOK, 2 * HEAD_DIM), F32),
        ],
        limit=60,
        flops=400_000_000_000,
        moved=8_000_000,
    )(
        doc_lengths, *here, *near, up4, theirs, theirs4
    )
    returned = [lax.ppermute(p, group, back[r]) for r, p in enumerate(mixed)]

    lin_out = halved(
        finish_kernel,
        out((rows, width), F32),
        1,
        (
            doc_lengths,
            decay_rate,
            lin_query,
            state,
            intra,
            lin_gate,
            norm_gain.reshape(1, width),
        ),
        (0, 1, 0, 1, 1, 1),
    )
    lin_out, *returned = lax.optimization_barrier((lin_out, *returned))
    sm_out = call(place_kernel, out((rows, width), F32), 3)(doc_lengths, *returned)
    return (lin_out, sm_out)


def solution(mesh):
    sizes = mesh.shape
    ring = 4
    inner = Mesh(
        mesh.devices.reshape(ring, sizes["context"] // ring, sizes["head"], sizes["dp"]),
        ("y", "z", "head", "dp"),
    )
    tokens = ("dp", "y", "z")
    wide = P(tokens, "head")
    in_specs = (
        wide,
        wide,
        wide,
        wide,
        P("head", tokens),
        P("head"),
        wide,
        wide,
        wide,
        P("dp"),
    )
    return jax.shard_map(
        shards, mesh=inner, in_specs=in_specs, out_specs=(wide, wide), check_vma=False
    )
```

```python
import functools
import math

import jax
import jax.numpy as jnp
import numpy as np
from jax import lax
from jax.experimental import pallas as pl
from jax.experimental.pallas import tpu as pltpu
from jax.sharding import Mesh, PartitionSpec as P

HEAD_DIM = 128
ROT_DIM = 64
TOK = 128
DOCS = 16
CHUNK = 512
PIECES = (0, 1, -1, 2, -2, 3, -3, 4)
NEG = -1e30
GROUP = 8
QUERIES = GROUP * HEAD_DIM
ROPE_BASE = 10000000.0
NORM_EPS = 1e-05
F32 = jnp.float32
BF16 = jnp.bfloat16

INVERSE = np.power(
    ROPE_BASE, -(2.0 * np.arange(ROT_DIM // 2, dtype=np.float64)) / ROT_DIM
).astype(np.float32)

VMEM = pl.BlockSpec(memory_space=pltpu.VMEM)
SMEM = pl.BlockSpec(memory_space=pltpu.SMEM)


def built(kernel, out_shape, shapes, scratch=(), flops=1000, moved=1000, limit=20, left=0):
    def whole(shape):
        return pl.BlockSpec(shape, lambda i: (0,) * len(shape))

    many = isinstance(out_shape, (tuple, list))
    return pl.pallas_call(
        kernel,
        out_shape=out_shape,
        grid=(1,),
        in_specs=[SMEM]
        + [whole(shape) for shape in shapes[: len(shapes) - left]]
        + [pl.BlockSpec(memory_space=pl.ANY)] * left,
        out_specs=[whole(o.shape) for o in out_shape] if many else whole(out_shape.shape),
        scratch_shapes=list(scratch),
        compiler_params=pltpu.CompilerParams(vmem_limit_bytes=limit << 20),
        cost_estimate=pl.CostEstimate(
            flops=flops, bytes_accessed=moved, transcendentals=0
        ),
    )


def halved(kernel, out, out_axis, arrays, axes):
    def half(shape, axis):
        block = tuple(n // 2 if d == axis else n for d, n in enumerate(shape))
        return pl.BlockSpec(
            block, lambda i: tuple(i if d == axis else 0 for d in range(len(shape)))
        )

    return pl.pallas_call(
        kernel,
        out_shape=out,
        grid=(2,),
        in_specs=[SMEM] + [half(a.shape, axis) for a, axis in zip(arrays[1:], axes)],
        out_specs=half(out.shape, out_axis),
        compiler_params=pltpu.CompilerParams(vmem_limit_bytes=60 << 20),
        cost_estimate=pl.CostEstimate(flops=1000, bytes_accessed=1000, transcendentals=0),
    )(*arrays)


def call(kernel, out_shape, n_in, **options):
    def run(lengths, *arrays):
        return built(kernel, out_shape, [a.shape for a in arrays], **options)(lengths, *arrays)

    return run


def halves(x):
    high = x.astype(BF16)
    return high, (x - high.astype(F32)).astype(BF16)


def dot(a, b, ca, cb):
    return lax.dot_general(a, b, (((ca,), (cb,)), ((), ())), preferred_element_type=F32)


def dot3(a, b, ca, cb):
    ah, al = halves(a)
    bh, bl = halves(b)
    return dot(ah, bh, ca, cb) + (dot(ah, bl, ca, cb) + dot(al, bh, ca, cb))


def begins_of(lengths_ref, tokens):
    begin = jnp.zeros_like(tokens)
    start = jnp.int32(0)
    for d in range(DOCS - 1):
        start = start + lengths_ref[d]
        begin = jnp.where(tokens >= start, start, begin)
    return begin


def begin_scalar(lengths_ref, token):
    begin = jnp.int32(0)
    start = jnp.int32(0)
    for d in range(DOCS - 1):
        start = start + lengths_ref[d]
        begin = jnp.where(token >= start, start, begin)
    return begin


def block_of():
    return lax.axis_index("y") * lax.axis_size("z") + lax.axis_index("z")


def sent_in(r):
    return (lax.axis_index("y") // 2 + r) % 2


def row_of(r, core):
    return 2 * ((lax.axis_index("y") - r + 2) % 2) + core


def rope_tables(lengths_ref, inverse_ref, first):
    rows = first + lax.broadcasted_iota(jnp.int32, (TOK, HEAD_DIM), 0)
    lane = lax.broadcasted_iota(jnp.int32, (TOK, HEAD_DIM), 1)
    position = (rows - begins_of(lengths_ref, rows)).astype(F32)
    angle = position * inverse_ref[...]
    rotated = lane < ROT_DIM
    cosine = jnp.where(rotated, jnp.cos(angle), 1.0)
    sine = jnp.sin(angle)
    low = jnp.where(lane < ROT_DIM // 2, -sine, 0.0)
    high = jnp.where(rotated & (lane >= ROT_DIM // 2), sine, 0.0)
    return cosine, low, high


def rotated(x, tables):
    cosine, low, high = tables
    half = ROT_DIM // 2
    return (
        x * cosine
        + pltpu.roll(x, HEAD_DIM - half, 1) * low
        + pltpu.roll(x, half, 1) * high
    )


def kv_kernel(lengths_ref, inverse_ref, key_ref, value_ref, tables_ref, *pieces):
    tables = rope_tables(lengths_ref, inverse_ref, block_of() * TOK)
    for i in range(3):
        tables_ref[i] = tables[i]
    for r in range(2):
        at = pl.multiple_of(sent_in(r) * HEAD_DIM, HEAD_DIM)
        pieces[r][:, :HEAD_DIM] = rotated(key_ref[:, pl.ds(at, HEAD_DIM)], tables)
        pieces[r][:, HEAD_DIM:] = value_ref[:, pl.ds(at, HEAD_DIM)]


def query_kernel(lengths_ref, tables_ref, query_ref, *pieces):
    tables = [tables_ref[i] for i in range(3)]
    scale = math.log2(math.e) / math.sqrt(HEAD_DIM)
    for r in range(2):
        for n in range(GROUP):
            at = pl.multiple_of(sent_in(r) * QUERIES + n * HEAD_DIM, HEAD_DIM)
            x = query_ref[:, pl.ds(at, HEAD_DIM)]
            pieces[r][:, n * HEAD_DIM : (n + 1) * HEAD_DIM] = rotated(x, tables) * scale


def pack(copies, landing, kcat, vcat):
    z, zs = lax.axis_index("z"), lax.axis_size("z")
    core = lax.axis_index("head")
    for i in range(8):
        source = (z - PIECES[i] + zs) % zs
        for own in (True, False):
            copies[i if own else 8 + i].wait()
            for r in range(2):
                x = landing[i if own else 8 + i, r]
                row = row_of(r, core if own else 1 - core)
                at = pl.multiple_of((row * zs + source) * TOK, TOK)
                high, low = halves(x[:, :HEAD_DIM])
                kcat[pl.ds(at, TOK), 0:128] = high
                kcat[pl.ds(at, TOK), 128:256] = high
                kcat[pl.ds(at, TOK), 256:384] = low
                high, low = halves(x[:, HEAD_DIM:])
                vcat[pl.ds(at, TOK), 0:128] = high
                vcat[pl.ds(at, TOK), 128:256] = low


def softmax_kernel(lengths_ref, *refs):
    queries, pieces, outs = refs[:2], refs[2:12], refs[12:14]
    kcat, vcat = refs[14:16]
    landing, sems = refs[-2:]
    sources = [*pieces[:8], *[pieces[8].at[i] for i in range(7)], pieces[9]]
    copies = [
        pltpu.make_async_copy(source, landing.at[i], sems.at[i])
        for i, source in enumerate(sources)
    ]
    for copy in copies:
        copy.start()
    pack(copies, landing, kcat, vcat)
    for r in range(2):
        attend(r, lengths_ref, queries[r], kcat, vcat, outs[r], *refs[16:-2])


def attend(r, lengths_ref, query_ref, kcat, vcat, out_ref, *scratch):
    qcat, s_ref, m_ref, l_ref, acc_ref = scratch
    block = row_of(r, lax.axis_index("head")) * lax.axis_size("z") + lax.axis_index("z")
    first = block * TOK
    for n in range(GROUP):
        qh, ql = halves(query_ref[:, n * HEAD_DIM : (n + 1) * HEAD_DIM])
        qcat[n * TOK : (n + 1) * TOK, 0:128] = qh
        qcat[n * TOK : (n + 1) * TOK, 128:256] = ql
        qcat[n * TOK : (n + 1) * TOK, 256:384] = qh
    low = begin_scalar(lengths_ref, first) // CHUNK
    high = first // CHUNK + 1
    inner = (begin_scalar(lengths_ref, first + TOK - 1) + CHUNK - 1) // CHUNK
    inner = jnp.minimum(inner, high)
    outer = jnp.maximum(inner, high - 1)
    m_ref[...] = jnp.full_like(m_ref, NEG)
    l_ref[...] = jnp.zeros_like(l_ref)
    acc_ref[...] = jnp.zeros_like(acc_ref)

    def score(j, masked):
        at = pl.multiple_of(j * CHUNK, CHUNK)
        s = dot(qcat[...], kcat[pl.ds(at, CHUNK), :], 1, 1)
        if masked:
            rows = first + lax.broadcasted_iota(jnp.int32, (TOK, CHUNK), 0)
            keys = at + lax.broadcasted_iota(jnp.int32, (TOK, CHUNK), 1)
            begin = begins_of(
                lengths_ref, first + lax.broadcasted_iota(jnp.int32, (TOK, 1), 0)
            )
            visible = (keys >= begin) & (keys <= rows)
            s = jnp.where(visible[None], s.reshape(GROUP, TOK, CHUNK), NEG)
            s = s.reshape(GROUP * TOK, CHUNK)
        s_ref[j] = s
        top = s[:, :HEAD_DIM]
        for i in range(1, CHUNK // HEAD_DIM):
            top = jnp.maximum(top, s[:, i * HEAD_DIM : (i + 1) * HEAD_DIM])
        m_ref[...] = jnp.maximum(m_ref[...], top)

    pl.loop(low, inner)(lambda j: score(j, True))
    pl.loop(inner, outer)(lambda j: score(j, False))
    pl.loop(outer, high)(lambda j: score(j, True))

    top = jnp.max(m_ref[...], axis=1, keepdims=True)
    m_ref[...] = jnp.broadcast_to(top, m_ref.shape)

    def mix(j):
        at = pl.multiple_of(j * CHUNK, CHUNK)
        top = m_ref[...]
        highs, lows, total = [], [], l_ref[...]
        for i in range(CHUNK // HEAD_DIM):
            p = jnp.exp2(s_ref[j, :, i * HEAD_DIM : (i + 1) * HEAD_DIM] - top)
            total = total + p
            ph, pl_ = halves(p)
            highs.append(ph)
            lows.append(pl_)
        l_ref[...] = total
        v = vcat[pl.ds(at, CHUNK), :]
        p = jnp.concatenate(highs + lows, axis=1)
        acc_ref[...] += dot(p, jnp.concatenate([v, v], axis=0), 1, 0)

    pl.loop(low, high)(mix)

    total = jnp.sum(l_ref[...], axis=1, keepdims=True)
    mixed = (acc_ref[:, :HEAD_DIM] + acc_ref[:, HEAD_DIM:]) / total
    for n in range(GROUP):
        out_ref[:, n * HEAD_DIM : (n + 1) * HEAD_DIM] = mixed[n * TOK : (n + 1) * TOK]


def place_kernel(lengths_ref, *refs):
    pieces, out_ref = refs[:2], refs[2]
    for r in range(2):
        at = pl.multiple_of(sent_in(r) * QUERIES, QUERIES)
        out_ref[:, pl.ds(at, QUERIES)] = pieces[r][...]


def thirds(x):
    high = x.astype(BF16)
    rest = x - high.astype(F32)
    mid = rest.astype(BF16)
    return high, mid, (rest - mid.astype(F32)).astype(BF16)


def dot6(a, b, ca, cb):
    ah, am, al = thirds(a)
    bh, bm, bl = thirds(b)
    return dot(
        jnp.concatenate([ah, am, ah, al, am, ah], axis=ca),
        jnp.concatenate([bl, bm, bm, bh, bh, bh], axis=cb),
        ca,
        cb,
    )


def decay_columns(rate_ref):
    t = lax.broadcasted_iota(jnp.int32, (TOK, TOK), 0)
    s = lax.broadcasted_iota(jnp.int32, (TOK, TOK), 1)
    lower = jnp.where(s <= t, 1.0, 0.0).astype(BF16)
    parts = [dot(lower, x, 1, 1) for x in thirds(-rate_ref[...])]
    return parts[0] + (parts[1] + parts[2])


def decay_rows(rate_ref):
    s = lax.broadcasted_iota(jnp.int32, (TOK, TOK), 0)
    t = lax.broadcasted_iota(jnp.int32, (TOK, TOK), 1)
    upper = jnp.where(s <= t, 1.0, 0.0).astype(BF16)
    parts = [dot(x, upper, 1, 0) for x in thirds(-rate_ref[...])]
    return parts[0] + (parts[1] + parts[2])


def state_kernel(lengths_ref, rate_ref, key_ref, value_ref, out_ref):
    heads = rate_ref.shape[0]
    first = block_of() * TOK
    tail = begin_scalar(lengths_ref, first + TOK - 1)
    columns = decay_columns(rate_ref)
    rows = first + lax.broadcasted_iota(jnp.int32, (TOK, heads), 0)
    end = columns[TOK - 1 : TOK, :]
    weight = jnp.where(
        rows >= tail, jnp.exp(jnp.where(rows >= tail, end - columns, 0.0)), 0.0
    )
    carried = jnp.where(tail < first, jnp.exp(end), 0.0)
    half = HEAD_DIM // 2
    for h in range(heads):
        lanes = slice(h * HEAD_DIM, (h + 1) * HEAD_DIM)
        k = key_ref[:, lanes] * weight[:, h : h + 1]
        kh, kl = halves(k)
        vh, vl = halves(value_ref[:, lanes])
        inner = dot(
            jnp.concatenate([kh, kh, kl], axis=0),
            jnp.concatenate([vh, vl, vh], axis=0),
            0,
            0,
        )
        kept = jnp.broadcast_to(carried[:, h : h + 1], (8, HEAD_DIM))
        for i in range(2):
            out_ref[2 * h + i, :half] = inner[i * half : (i + 1) * half]
            out_ref[2 * h + i, half:] = kept


def prefix_kernel(lengths_ref, in_ref, out_ref):
    blocks, half = out_ref.shape[0], out_ref.shape[1]
    state = jnp.zeros(out_ref.shape[1:], F32)
    for i in range(blocks):
        out_ref[i] = state
        if i < blocks - 1:
            state = in_ref[i, half : half + 1, :] * state + in_ref[i, :half, :]


def intra_kernel(lengths_ref, rate_ref, query_ref, key_ref, value_ref, out_ref):
    heads = rate_ref.shape[0]
    first = block_of() * TOK
    columns = decay_columns(rate_ref)
    across = decay_rows(rate_ref)
    t = first + lax.broadcasted_iota(jnp.int32, (TOK, TOK), 0)
    s = first + lax.broadcasted_iota(jnp.int32, (TOK, TOK), 1)
    visible = (s <= t) & (s >= begins_of(lengths_ref, t))
    for h in range(heads):
        lanes = slice(h * HEAD_DIM, (h + 1) * HEAD_DIM)
        gap = jnp.where(visible, columns[:, h : h + 1] - across[h : h + 1, :], 0.0)
        weight = jnp.where(visible, jnp.exp(gap), 0.0)
        scores = dot6(query_ref[:, lanes], key_ref[:, lanes], 1, 1) * weight
        sh, sl = halves(scores)
        vh, vl = halves(value_ref[:, lanes])
        out_ref[:, lanes] = dot(
            jnp.concatenate([sh, sl, sh], axis=1), jnp.concatenate([vh, vh, vl], axis=0), 1, 0
        )


def finish_kernel(
    lengths_ref, rate_ref, query_ref, state_ref, intra_ref, gate_ref, gain_ref, out_ref
):
    heads = rate_ref.shape[0]
    first = block_of() * TOK
    columns = decay_columns(rate_ref)
    rows = first + lax.broadcasted_iota(jnp.int32, (TOK, heads), 0)
    carried = begins_of(lengths_ref, rows) < first
    reach = jnp.where(carried, jnp.exp(columns), 0.0)
    for h in range(heads):
        lanes = slice(h * HEAD_DIM, (h + 1) * HEAD_DIM)
        x = intra_ref[:, lanes] + dot3(query_ref[:, lanes], state_ref[h], 1, 0) * reach[
            :, h : h + 1
        ]
        mean = jnp.mean(x * x, axis=1, keepdims=True)
        normed = x / jnp.sqrt(mean + NORM_EPS)
        gate = 1.0 / (1.0 + jnp.exp(-gate_ref[:, lanes]))
        out_ref[:, lanes] = normed * gain_ref[:, lanes] * gate


def shards(
    lin_query,
    lin_key,
    lin_value,
    lin_gate,
    decay_rate,
    norm_gain,
    sm_query,
    sm_key,
    sm_value,
    doc_lengths,
):
    rows, width = lin_query.shape
    heads = width // HEAD_DIM
    ys, zs = lax.axis_size("y"), lax.axis_size("z")
    blocks = ys * zs
    group = ("y", "head")
    out = jax.ShapeDtypeStruct
    forth, back = [], []
    for r in range(2):
        pairs = [
            (2 * y + h, 2 * (2 * h + (y // 2 + r) % 2) + y % 2)
            for y in range(ys)
            for h in range(2)
        ]
        forth.append(pairs)
        back.append([(b, a) for a, b in pairs])

    sliced = halved(
        state_kernel,
        out((blocks, HEAD_DIM // 2 + 8, HEAD_DIM), F32),
        0,
        (doc_lengths, decay_rate, lin_key, lin_value),
        (0, 1, 1),
    )
    arrived = lax.all_to_all(sliced, ("y", "z"), 0, 0, tiled=True)

    inverse = np.zeros((1, HEAD_DIM), np.float32)
    inverse[0, :ROT_DIM] = np.tile(INVERSE, 2)
    sm_key, sliced = lax.optimization_barrier((sm_key, sliced))
    tables, *kv_pieces = call(
        kv_kernel,
        [out((3, rows, HEAD_DIM), F32)] + [out((rows, 2 * HEAD_DIM), F32)] * 2,
        4,
        limit=60,
    )(doc_lengths, jnp.asarray(inverse), sm_key, sm_value)
    kv_here = [lax.ppermute(p, group, forth[r]) for r, p in enumerate(kv_pieces)]

    up = [(i, (i + 1) % zs) for i in range(zs)]
    down = [(b, a) for a, b in up]
    own = jnp.stack(kv_here)
    up1 = lax.ppermute(own, "z", up)
    down1 = lax.ppermute(own, "z", down)

    sm_query, lin_query, own = lax.optimization_barrier((sm_query, lin_query, own))
    q_pieces = call(query_kernel, [out((rows, QUERIES), F32)] * 2, 3, limit=60)(
        doc_lengths, tables, sm_query
    )
    here = [lax.ppermute(p, group, forth[r]) for r, p in enumerate(q_pieces)]
    intra = call(intra_kernel, out((rows, width), F32), 5)(
        doc_lengths, decay_rate, lin_query, lin_key, lin_value
    )
    up1, down1, arrived, intra = lax.optimization_barrier((up1, down1, arrived, intra))
    up2 = lax.ppermute(up1, "z", up)
    down2 = lax.ppermute(down1, "z", down)
    prefixes = call(prefix_kernel, out((blocks, HEAD_DIM // 2, HEAD_DIM), F32), 2)(
        doc_lengths, arrived
    )
    up2, down2, prefixes, *here = lax.optimization_barrier((up2, down2, prefixes, *here))
    up3 = lax.ppermute(up2, "z", up)
    down3 = lax.ppermute(down2, "z", down)
    up3, down3, prefixes = lax.optimization_barrier((up3, down3, prefixes))
    up4 = lax.ppermute(up3, "z", up)
    cross = [
        (2 * i + c, 2 * ((i - 1) % zs) + 1 - c) for i in range(zs) for c in range(2)
    ]
    theirs4 = lax.ppermute(down3, ("z", "head"), cross)
    near = [own, up1, down1, up2, down2, up3, down3]
    theirs = lax.ppermute(jnp.stack(near), "head", [(0, 1), (1, 0)])

    state = lax.all_to_all(prefixes, ("y", "z"), 0, 0, tiled=True)
    state = state.reshape(heads, HEAD_DIM, HEAD_DIM)

    keys = blocks * TOK
    mixed = call(
        softmax_kernel,
        [out((rows, QUERIES), F32)] * 2,
        13,
        scratch=[
            pltpu.VMEM((keys, 384), BF16),
            pltpu.VMEM((keys, 256), BF16),
            pltpu.VMEM((GROUP * TOK, 384), BF16),
            pltpu.VMEM((keys // CHUNK, GROUP * TOK, CHUNK), F32),
            pltpu.VMEM((GROUP * TOK, HEAD_DIM), F32),
            pltpu.VMEM((GROUP * TOK, HEAD_DIM), F32),
            pltpu.VMEM((GROUP * TOK, 2 * HEAD_DIM), F32),
            pltpu.VMEM((16, 2, TOK, 2 * HEAD_DIM), F32),
            pltpu.SemaphoreType.DMA((16,)),
        ],
        limit=60,
        left=10,
        flops=400_000_000_000,
        moved=8_000_000,
    )(
        doc_lengths, *here, *near, up4, theirs, theirs4
    )
    returned = [lax.ppermute(p, group, back[r]) for r, p in enumerate(mixed)]

    lin_out = halved(
        finish_kernel,
        out((rows, width), F32),
        1,
        (
            doc_lengths,
            decay_rate,
            lin_query,
            state,
            intra,
            lin_gate,
            norm_gain.reshape(1, width),
        ),
        (0, 1, 0, 1, 1, 1),
    )
    lin_out, *returned = lax.optimization_barrier((lin_out, *returned))
    sm_out = call(place_kernel, out((rows, width), F32), 3)(doc_lengths, *returned)
    return (lin_out, sm_out)


def solution(mesh):
    sizes = mesh.shape
    ring = 4
    inner = Mesh(
        mesh.devices.reshape(ring, sizes["context"] // ring, sizes["head"], sizes["dp"]),
        ("y", "z", "head", "dp"),
    )
    tokens = ("dp", "y", "z")
    wide = P(tokens, "head")
    in_specs = (
        wide,
        wide,
        wide,
        wide,
        P("head", tokens),
        P("head"),
        wide,
        wide,
        wide,
        P("dp"),
    )
    return jax.shard_map(
        shards, mesh=inner, in_specs=in_specs, out_specs=(wide, wide), check_vma=False
    )
```
